256 devices in a mesh: dom: 64 (over z, y, core), bin: 4 (over x).
Axes of the slice: x: 4, y: 4, z: 8, core: 2. Of those that a mesh axis runs over, the one named last changes fastest.
Arguments:
- field_in: float32 [8, 1048576], P(None, ('dom', 'bin')), may hold values from -6 to 6
- heading_in: float32 [3, 1048576], P(None, ('dom', 'bin')), may hold values from -3 to 3
- launch_domain: int32 [1048576, 1], P(('dom', 'bin')), may hold values from 0 to 63; in each aligned block of 4096 rows (0 to 4095, 4096 to 8191, ...) at most 128 rows name the same one
- hop_domain: int32 [3, 1048576, 1], P(None, ('dom', 'bin')), may hold values from 0 to 63; in each aligned block of 4096 rows (0 to 4095, 4096 to 8191, ..., all dimensions but the last counted through in order) at most 128 rows name the same one
- hit_facet: int32 [4, 1048576], P(None, ('dom', 'bin')), may hold values from 0 to 8191
- path_phase: float32 [4, 1048576], P(None, ('dom', 'bin')), may hold values from -3.140625 to 3.140625
- facet_polar: float32 [524288], P('dom'), may hold values from -3.140625 to 3.140625
- facet_azimuth: float32 [524288], P('dom'), may hold values from -3.140625 to 3.140625
- facet_tilt: float32 [524288], P('dom'), may hold values from -3.140625 to 3.140625
- surface_resistance: float32 [524288], P('dom'), may hold values from 0.2 to 5
- surface_reactance: float32 [524288], P('dom'), may hold values from -1 to 1
- kernel: bfloat16 [2, 524288, 1024], P(None, ('dom', 'bin')), may hold values from -0.00390625 to 0.00390625
Outputs:
- far_field: float32 [8, 1024], P(None, ('dom', 'bin'))
- exit_field: float32 [8, 1048576], P(None, ('dom', 'bin'))
The draws below stay inside these ranges and needn't reach their ends.
Inputs may be any that keep to these rules, and one draw needn't show every extreme that they name: `launch_domain`: among the 4096 tubes launched from one device (aligned blocks of the tube dimension), each domain is named at most 128 times in each bounce, and exactly 128 times by some domain in some blocks. `hop_domain`: among the 4096 tubes launched from one device, each domain is named at most 128 times in each bounce, and exactly 128 times by some domain in some blocks.
All inputs are finite; a program needn't handle non-finite values.
Results may differ from the reference program's by a relative error of at most 0.0029.
Values sent between devices are 32-bit elements; how exact they have to be, the bound alone decides.
A program may use at most 128 MiB of HBM per device.

```python
import math
import jax
import jax.numpy as jnp
import numpy as np

TUBES_DEV = 4096
BOUNCES = 4
FAC = 8192
BINS = 1024
TUBES = 1048576
FACETS = 524288
CAP = 128
N_DOM = 64


def touch_ends(drawn, stream_key, least, top_value):
    longest = drawn.shape.index(max(drawn.shape))
    spots = []
    for shift in (0, 1):
        where = [jax.random.randint(jax.random.fold_in(stream_key, axis), (), 0, length) for axis, length in enumerate(drawn.shape)]
        where[longest] = (where[longest] + shift) % drawn.shape[longest]
        spots.append(tuple(where))
    return drawn.at[spots[0]].set(least).at[spots[1]].set(top_value)


def with_spikes(drawn, own_key, source, target, blocks, factor):
    owner, partner = [(jnp.arange(drawn.shape[axis_at]) // (drawn.shape[axis_at] // blocks)).reshape([-1 if axis == axis_at else 1 for axis in range(drawn.ndim)]) for axis_at in (source, target)]
    chosen = jax.random.permutation(own_key, blocks)[partner]
    strong = (owner == chosen) | (owner == (partner + blocks // 2) % blocks)
    return jnp.where(strong, factor * drawn, drawn)


def steps_of(key, extent, shards, smallest, largest):
    gain, own = 1.0, jax.random.fold_in(key, 6)
    for dim, parts in shards:
        steps = jnp.exp(jax.random.uniform(jax.random.fold_in(own, dim), (parts,), jnp.float32, smallest / len(shards), largest / len(shards)))
        gain = gain * jnp.repeat(steps, extent[dim] // parts).reshape([-1 if axis == dim else 1 for axis in range(len(extent))])
    return gain


def deal_out(key, own, number, rows, count, top, bound, skew):
    ranking = jax.random.permutation(key, count)
    packed, usual = portions_of(count, rows * top, bound, skew, True), portions_of(count, rows * top, bound, skew, False)
    places = jnp.arange(count)

    def named(sizes, offset_by):
        used = int((sizes > 0).sum())
        fixed = max(1, used // 4)
        shifted = fixed + (places - fixed + offset_by * (used - fixed)) % max(1, count - fixed)
        return jnp.zeros((count,), jnp.int32).at[ranking[jnp.where(places < fixed, places, shifted)]].set(jnp.asarray(sizes, jnp.int32))

    sizes = jnp.where(number % 4 == 0, named(packed, number // 4), named(usual, number - number // 4 - 1))
    mixed = jax.random.permutation(jax.random.fold_in(own, 3), count)
    donor, sink = mixed[0:count // 2 * 2:2], mixed[1:count // 2 * 2:2]
    margin = jnp.minimum(sizes[donor] - 1, bound - sizes[sink]) // 2
    margin = jnp.where((donor == ranking[0]) | (sink == ranking[0]) | (sizes[sink] == 0), 0, jnp.maximum(margin, 0))
    shifted = jax.random.randint(jax.random.fold_in(own, 4), (count // 2,), 0, 1 << 20) % (margin + 1)
    sizes = sizes.at[donor].add(-shifted).at[sink].add(shifted)
    labels = jnp.searchsorted(jnp.cumsum(sizes), jnp.arange(rows * top), side="right").astype(jnp.int32)
    table = labels.reshape(top, rows).T
    table = table[jax.random.permutation(jax.random.fold_in(own, 1), rows)]
    offset_by = jax.random.randint(jax.random.fold_in(own, 2), (rows, 1), 0, top)
    return jnp.take_along_axis(table, (jnp.arange(top)[None, :] + offset_by) % top, axis=1)


def portions_of(number_of, total, reach, slope, full):
    weights = [(1 << 20) // math.isqrt(standing ** slope) + 1 for standing in range(1, number_of + 1)]
    largest = reach if full else min(reach, max(-(-total // number_of), total * weights[0] // sum(weights)))
    least = 1 if total - largest >= number_of - 1 else 0
    counts, rest = [largest] + [least] * (number_of - 1), total - largest - least * (number_of - 1)
    while rest > 0:
        free = [i for i in range(1, number_of) if counts[i] < largest] or [i for i in range(1, number_of) if counts[i] < reach]
        whole, budget = sum([weights[i] for i in free]), rest
        for i in free:
            addition = min(reach - counts[i], max(1, budget * weights[i] // whole), rest)
            counts[i] = counts[i] + addition
            rest = rest - addition
    return np.array(counts)


def noise(key, dims, width, reach, split=(), dtype=jnp.bfloat16):
    values = width * jax.random.normal(key, dims, jnp.float32)
    if split:
        values = values * steps_of(key, dims, split, -0.22, 0.18)
    return jnp.clip(values, -reach, reach).astype(dtype)


def bell_draw_with(rng, extent, scale, most, split, heavy, held_as=jnp.bfloat16):
    values = scale * jax.random.normal(rng, extent, jnp.float32)
    if split:
        values = values * steps_of(rng, extent, split, -0.22, 0.18)
    return jnp.clip(with_spikes(values, jax.random.fold_in(rng, 3), *heavy), -most, most).astype(held_as)


def setup_inputs(seed: int = 0) -> dict:
    seeds = jax.random.split(jax.random.key(seed), 13)
    field_in = noise(seeds[0], (8, TUBES), 1.0, 6.0, ((1, 256),), jnp.float32)
    heading_in = noise(seeds[1], (3, TUBES), 0.6, 3.0, ((1, 256),), jnp.float32)
    launch_domain_keys = jax.random.split(jax.random.fold_in(seeds[2], 1), TUBES // TUBES_DEV)
    launch_domain_turns = jax.random.permutation(jax.random.fold_in(seeds[2], 3), TUBES // TUBES_DEV)
    launch_domain = jax.vmap(lambda own, number: deal_out(jax.random.fold_in(seeds[2], 2), own, number, TUBES_DEV, N_DOM, 1, CAP, 2))(launch_domain_keys, launch_domain_turns).reshape((TUBES, 1))
    hop_domain_keys = jax.random.split(jax.random.fold_in(seeds[3], 1), (BOUNCES - 1) * TUBES // TUBES_DEV)
    hop_domain_turns = jax.random.permutation(jax.random.fold_in(seeds[3], 3), (BOUNCES - 1) * TUBES // TUBES_DEV)
    hop_domain = jax.vmap(lambda own, number: deal_out(jax.random.fold_in(seeds[3], 2), own, number, TUBES_DEV, N_DOM, 1, CAP, 2))(hop_domain_keys, hop_domain_turns).reshape((BOUNCES - 1, TUBES, 1))
    hit_facet = touch_ends(jax.random.randint(seeds[4], (BOUNCES, TUBES), 0, FAC), jax.random.fold_in(seeds[4], 1), 0, FAC - 1).astype(jnp.int32)
    path_phase = jnp.clip(jax.random.uniform(seeds[5], (BOUNCES, TUBES), jnp.float32, -3.140625, 3.140625), -3.140625, 3.140625)
    facet_polar = jnp.clip(jax.random.uniform(seeds[6], (FACETS,), jnp.float32, -3.140625, 3.140625), -3.140625, 3.140625)
    facet_azimuth = jnp.clip(jax.random.uniform(seeds[7], (FACETS,), jnp.float32, -3.140625, 3.140625), -3.140625, 3.140625)
    facet_tilt = jnp.clip(jax.random.uniform(seeds[8], (FACETS,), jnp.float32, -3.140625, 3.140625), -3.140625, 3.140625)
    surface_resistance = jnp.clip(jnp.exp(math.log(5.0) - 3.218876 * jax.random.uniform(seeds[9], (FACETS,), jnp.float32) ** steps_of(seeds[9], (FACETS,), ((0, 64),), -0.2, 0.2)), 0.2, 5.0)
    surface_reactance = jnp.clip(jax.random.uniform(seeds[10], (FACETS,), jnp.float32, -1.0, 1.0) * steps_of(seeds[10], (FACETS,), ((0, 64),), -0.4, 0.0), -1.0, 1.0)
    kernel = bell_draw_with(seeds[11], (2, FACETS, BINS), (64 * FACETS) ** -0.5, 0.00390625, ((1, 256),), (1, 2, 256, 6.0))
    return {"field_in": field_in, "heading_in": heading_in, "launch_domain": launch_domain, "hop_domain": hop_domain, "hit_facet": hit_facet, "path_phase": path_phase, "facet_polar": facet_polar, "facet_azimuth": facet_azimuth, "facet_tilt": facet_tilt, "surface_resistance": surface_resistance, "surface_reactance": surface_reactance, "kernel": kernel}


def facet_frame(polar_angle, azimuth, tilt_angle, resistance, reactance):
    return jnp.stack([jnp.sin(polar_angle) * jnp.cos(azimuth), jnp.sin(polar_angle) * jnp.sin(azimuth), jnp.cos(polar_angle), resistance, reactance, jnp.cos(tilt_angle), jnp.sin(tilt_angle)], axis=0)


def divide(top_real, top_imag, low_real, low_imag):
    modulus = low_real * low_real + low_imag * low_imag
    return (top_real * low_real + top_imag * low_imag) / modulus, (top_imag * low_real - top_real * low_imag) / modulus


def turn_phase(tube_field, phase_angle):
    phase_cos = jnp.cos(phase_angle)
    phase_sin = jnp.sin(phase_angle)
    return jnp.concatenate([phase_cos * tube_field[0:4] - phase_sin * tube_field[4:8], phase_sin * tube_field[0:4] + phase_cos * tube_field[4:8]], axis=0)


def reflect(tube_field, heading, facet_rows):
    normal = facet_rows[0:3]
    incidence = jnp.sum(heading * normal, axis=0)
    cosine = jnp.abs(incidence)
    eta_real = facet_rows[3]
    eta_imag = facet_rows[4]
    tilt_cos = facet_rows[5]
    tilt_sin = facet_rows[6]
    te_real, te_imag = divide(cosine - eta_real, -eta_imag, cosine + eta_real, eta_imag)
    tm_real, tm_imag = divide(eta_real * cosine - 1.0, eta_imag * cosine, eta_real * cosine + 1.0, eta_imag * cosine)
    upper_real = tilt_cos * tube_field[0:2] + tilt_sin * tube_field[2:4]
    lower_real = tilt_cos * tube_field[2:4] - tilt_sin * tube_field[0:2]
    upper_imag = tilt_cos * tube_field[4:6] + tilt_sin * tube_field[6:8]
    lower_imag = tilt_cos * tube_field[6:8] - tilt_sin * tube_field[4:6]
    result = jnp.concatenate([te_real * upper_real - te_imag * upper_imag, tm_real * lower_real - tm_imag * lower_imag, te_real * upper_imag + te_imag * upper_real, tm_real * lower_imag + tm_imag * lower_real], axis=0)
    turned = heading - 2.0 * incidence * normal
    return result, turned


def reference(field_in, heading_in, launch_domain, hop_domain, hit_facet, path_phase, facet_polar, facet_azimuth, facet_tilt, surface_resistance, surface_reactance, kernel):
    frame_all = facet_frame(facet_polar, facet_azimuth, facet_tilt, surface_resistance, surface_reactance)
    tube_field = field_in
    heading = heading_in
    facet_sums = jnp.zeros((8, FACETS), jnp.float32)
    for bounce in range(BOUNCES):
        if bounce == 0:
            target = launch_domain[:, 0].astype(jnp.int32)
        else:
            target = hop_domain[bounce - 1, :, 0].astype(jnp.int32)
        global_facet = (target * FAC + hit_facet[bounce].astype(jnp.int32)).astype(jnp.int32)
        phased = turn_phase(tube_field, path_phase[bounce])
        facet_rows = jnp.take(frame_all, global_facet, axis=1)
        tube_field, heading = reflect(phased, heading, facet_rows)
        facet_sums = facet_sums.at[:, global_facet].add(tube_field)
    rounded = facet_sums.astype(jnp.bfloat16)
    real_part = jnp.dot(rounded, kernel[0], preferred_element_type=jnp.float32)
    imag_part = jnp.dot(rounded, kernel[1], preferred_element_type=jnp.float32)
    far_field = jnp.concatenate([real_part[0:4] - imag_part[4:8], imag_part[0:4] + real_part[4:8]], axis=0)
    return far_field, tube_field
```

```python
import jax
import jax.numpy as jnp
from jax import lax
from jax.experimental import pallas as pl
from jax.experimental.pallas import tpu as pltpu
from jax.sharding import PartitionSpec as P

BOUNCES = 4
HALVES = 2
EACH = BOUNCES // HALVES
DOMS = 64
BINS = 4
CAP = 128
LANES = 128
ROWS = 32
PARAMS = 5
BATCH = 16
F32 = jnp.float32
BF16 = jnp.bfloat16
I32 = jnp.int32
MESH = pl.DeviceIdType.MESH
LAST = (((1,), (1,)), ((), ()))


def iota(shape, dim):
    return lax.broadcasted_iota(I32, shape, dim)


def narrow(x):
    return x.astype(F32).astype(BF16)


def split(x):
    big = x.astype(BF16)
    return big, (x - big.astype(F32)).astype(BF16)


def one_hot(rows, depth):
    count = narrow(iota((depth, LANES), 0))
    one, zero = jnp.ones((depth, LANES), BF16), jnp.zeros((depth, LANES), BF16)
    hot = [jnp.where(count == narrow(jnp.broadcast_to(r, (depth, LANES))), one, zero) for r in rows]
    return jnp.concatenate(hot, axis=1)


def sin_cos(x):
    turns = jnp.floor(x * 0.6366197723675814 + 0.5)
    r = x - turns * 1.5703125
    r = r - turns * 4.83826794896e-4
    z = r * r
    s = ((-1.9515295891e-4 * z + 8.3321608736e-3) * z - 1.6666654611e-1) * z * r + r
    c = ((2.443315711809948e-5 * z - 1.388731625493765e-3) * z + 4.166664568298827e-2) * z * z
    c = c - 0.5 * z + 1.0
    odd = jnp.abs(turns) == 1.0
    near = turns == 0.0
    sine = jnp.where(odd, turns * c, jnp.where(near, s, -s))
    cosine = jnp.where(odd, -turns * s, jnp.where(near, c, -c))
    return sine, cosine


def divide(top_real, top_imag, low_real, low_imag):
    scale = 1.0 / (low_real * low_real + low_imag * low_imag)
    return (
        (top_real * low_real + top_imag * low_imag) * scale,
        (top_imag * low_real - top_real * low_imag) * scale,
    )


def lookup(table, rows, store):
    size = 32 * PARAMS
    found = jnp.dot(table[...], one_hot([r & 255 for r in rows], 256), preferred_element_type=F32)
    found = found[:size] + found[size:]
    for i, r in enumerate(rows):
        hi = jnp.broadcast_to(r >> 8, (8, LANES))
        group, line = hi >> 3, hi & 7
        for p in range(PARAMS):
            f = [
                found[32 * p + 8 * q : 32 * p + 8 * q + 8, LANES * i : LANES * (i + 1)]
                for q in range(4)
            ]
            y = jnp.where(
                group < 2, jnp.where(group == 0, f[0], f[1]), jnp.where(group == 2, f[2], f[3])
            )
            y = jnp.take_along_axis(y, line, axis=0, mode="promise_in_bounds")
            store(i, p, y[0:1])


def gathered_sums(rows, tiles):
    half = iota((16, LANES), 0) >> 3
    zero = jnp.zeros((16, LANES), BF16)
    parts = ([], [])
    for r, f in zip(rows, tiles):
        big = f.astype(BF16).astype(F32)
        hi = narrow(jnp.broadcast_to(r >> 8, (16, LANES)) - half)
        masks = [hi == jnp.asarray(2 * k, BF16) for k in range(16)]
        for part, value in zip(parts, (big, f - big)):
            twice = jnp.concatenate([value, value], axis=0).astype(BF16)
            part.append(jnp.concatenate([jnp.where(m, twice, zero) for m in masks], axis=0))
    left = jnp.concatenate([jnp.concatenate(part, axis=1) for part in parts], axis=0)
    total = lax.dot_general(
        left, one_hot([r & 255 for r in rows], 256), LAST, preferred_element_type=F32
    )
    return total[:256] + total[256:]


def ranks(b, target, facet, ids_out, slots):
    block = 2 * LANES
    blocks = ROWS // 2
    after = iota((block, 2 * block), 0) <= iota((block, 2 * block), 1)
    after = jnp.where(after | (iota((block, 2 * block), 1) >= block), 1.0, 0.0).astype(BF16)
    carry = jnp.zeros((DOMS, block), F32)
    doms = [target[b, n : n + 1, :] for n in range(ROWS)]
    marks = [one_hot(doms[2 * j : 2 * j + 2], DOMS) for j in range(blocks)]
    counts = jnp.dot(jnp.concatenate(marks, axis=0), after, preferred_element_type=F32)
    zero = jnp.zeros((DOMS, block), BF16)
    left, places = [], []
    for j in range(blocks):
        count = counts[DOMS * j : DOMS * (j + 1)]
        place = marks[j].astype(F32) * (count[:, :block] + carry)
        place = jnp.sum(place, axis=0, keepdims=True).astype(I32) - 1
        carry = carry + count[:, block:]
        for w in range(2):
            n = 2 * j + w
            mine = place[:, LANES * w : LANES * (w + 1)]
            slots[b, n : n + 1, :] = doms[n] * CAP + mine
            places.append(mine)
        ids = jnp.concatenate([facet[b, 2 * j + w : 2 * j + w + 1, :] for w in range(2)], axis=1)
        left.append(
            jnp.concatenate(
                [
                    jnp.where(marks[j] > zero, narrow(jnp.broadcast_to(v, (DOMS, block))), zero)
                    for v in (ids >> 7, ids & 127)
                ],
                axis=0,
            )
        )
    packed = lax.dot_general(
        jnp.concatenate(left, axis=1), one_hot(places, CAP), LAST, preferred_element_type=F32
    ).astype(I32)
    ids_out[:, b, :] = packed[:DOMS] * 128 + packed[DOMS:]


def reflection(b, frame, phase, heading, coef):
    polar, azimuth, tilt, res, rea = (frame[p] for p in range(PARAMS))
    sin_p, cos_p = sin_cos(polar)
    sin_a, cos_a = sin_cos(azimuth)
    sin_t, cos_t = sin_cos(tilt)
    sin_f, cos_f = sin_cos(phase[b])
    normal = (sin_p * cos_a, sin_p * sin_a, cos_p)
    d = [heading[k] for k in range(3)]
    m = d[0] * normal[0] + d[1] * normal[1] + d[2] * normal[2]
    cosine = jnp.abs(m)
    te_r, te_i = divide(cosine - res, -rea, cosine + res, rea)
    rc, xc = res * cosine, rea * cosine
    tm_r, tm_i = divide(rc - 1.0, xc, rc + 1.0, xc)
    coef[0] = cos_t
    coef[1] = sin_t
    coef[2] = te_r * cos_f - te_i * sin_f
    coef[3] = te_r * sin_f + te_i * cos_f
    coef[4] = tm_r * cos_f - tm_i * sin_f
    coef[5] = tm_r * sin_f + tm_i * cos_f
    for k in range(3):
        heading[k] = d[k] - 2.0 * m * normal[k]


def reflect(coef, field):
    row = iota((8, LANES), 0)
    is_upper = (row & 2) == 0
    is_real = row < 4
    for n in range(ROWS):
        cos_t, sin_t, te_r, te_i, tm_r, tm_i = (
            jnp.broadcast_to(coef[k, n : n + 1, :], (8, LANES)) for k in range(6)
        )
        f = field[n]
        other = jnp.where(is_upper, pltpu.roll(f, 6, 0), -pltpu.roll(f, 2, 0))
        q = cos_t * f + sin_t * other
        turned = pltpu.roll(q, 4, 0)
        turned = jnp.where(is_real, -turned, turned)
        field[n] = jnp.where(is_upper, te_r, tm_r) * q + jnp.where(is_upper, te_i, tm_i) * turned


def main_kernel(
    target, facet, table, phase, heading_in, field_in, weights,
    far, exit_field,
    held, weight_sem,
    ids_send, ids_got, slots, rows_table,
    facts_send, facts_got, frame, heading, coef, field,
    fields_send, fields_got, sums, sums_got, partial, along_got, piece, last_got,
    ids_sems, facts_ssem, facts_rsem, fields_ssem, fields_rsem, sums_sems, along_sems, last_sems,
):
    me, my_bin = lax.axis_index("dom"), lax.axis_index("bin")
    z, y, core = me // 8, (me // 2) % 4, me % 2

    def partner(k):
        return ((z + k // 8) % 8) * 8 + ((y + (k // 2) % 4) % 4) * 2 + (core + k % 2) % 2

    def same_z(k):
        dom = z * 8 + ((y + (k // 2) % 4) % 4) * 2 + (core + k % 2) % 2
        return dom, (my_bin + k // 8) % BINS

    def send(source, landing, ssem, rsem, dom, bin_at):
        pltpu.make_async_remote_copy(
            src_ref=source, dst_ref=landing, send_sem=ssem, recv_sem=rsem,
            device_id=(dom, bin_at), device_id_type=MESH,
        ).start()

    def await_bytes(ref, sem):
        pltpu.make_async_copy(ref, ref, sem).wait()

    fetch = pltpu.make_async_copy(weights, held, weight_sem)
    fetch.start()
    barrier = pltpu.get_barrier_semaphore()

    @pl.loop(1, DOMS)
    def _(k):
        pl.semaphore_signal(barrier, inc=1, device_id=(partner(k), my_bin), device_id_type=MESH)

    @pl.loop(8, 32)
    def _(k):
        pl.semaphore_signal(barrier, inc=1, device_id=same_z(k), device_id_type=MESH)

    @pl.loop(0, BOUNCES)
    def _(b):
        ranks(b, target, facet, ids_send, slots)

    for k in range(3):
        heading[k] = heading_in[k]
    for n in range(ROWS):
        field[n] = field_in[:, n * LANES : (n + 1) * LANES]
    big, small = split(table[...])
    rows_table[: 32 * PARAMS] = big
    rows_table[32 * PARAMS :] = small

    pl.semaphore_wait(barrier, DOMS - 1 + 24)

    @pl.loop(1, DOMS)
    def _(k):
        dom = partner(k)
        send(ids_send.at[dom], ids_got.at[me], ids_sems.at[0], ids_sems.at[1], dom, my_bin)

    ids_got[me] = ids_send[me]
    await_bytes(ids_send.at[pl.ds(0, DOMS - 1)], ids_sems.at[1])

    senders = BATCH // EACH

    @pl.loop(0, HALVES)
    def _(h):
        @pl.loop(0, DOMS // senders)
        def _(g):
            doms = [partner(g * senders + i) for i in range(senders)]
            asked = [ids_got[dom, pl.ds(EACH * h + w, 1), :] for dom in doms for w in range(EACH)]

            def store(i, p, value):
                facts_send[h, doms[i // EACH], p, i % EACH : i % EACH + 1, :] = value

            lookup(rows_table, asked, store)
            for i in range(senders):

                @pl.when(g * senders + i > 0)
                def _():
                    send(
                        facts_send.at[h, doms[i]], facts_got.at[h, me],
                        facts_ssem.at[h], facts_rsem.at[h], doms[i], my_bin,
                    )

        facts_got[h, me] = facts_send[h, me]

    @pl.loop(0, BOUNCES)
    def _(b):
        h, w = b // EACH, b % EACH

        @pl.when(w == 0)
        def _():
            await_bytes(facts_send.at[h, pl.ds(0, DOMS - 1)], facts_rsem.at[h])

        for p in range(PARAMS):
            rows = [
                facts_got[h, pl.ds(j, 32, stride=2), p, pl.ds(w, 1), :].reshape(32, LANES)
                for j in range(2)
            ]
            big, small = split(jnp.concatenate(rows, axis=1))
            rows_table[32 * p : 32 * (p + 1)] = big
            rows_table[32 * (PARAMS + p) : 32 * (PARAMS + p + 1)] = small
        for part in range(ROWS // BATCH):

            def store(i, p, value, part=part):
                frame[p, part * BATCH + i : part * BATCH + i + 1, :] = value

            lookup(
                rows_table,
                [slots[b, n : n + 1, :] for n in range(part * BATCH, (part + 1) * BATCH)],
                store,
            )
        reflection(b, frame, phase, heading, coef)
        reflect(coef, field)
        total = None
        for part in range(ROWS // BATCH):
            lines = range(part * BATCH, (part + 1) * BATCH)
            more = gathered_sums([slots[b, n : n + 1, :] for n in lines], [field[n] for n in lines])
            total = more if total is None else total + more
        for hi in range(32):
            fields_send[2 * hi, b] = total[8 * hi : 8 * hi + 8, :LANES]
            fields_send[2 * hi + 1, b] = total[8 * hi : 8 * hi + 8, LANES:]

        @pl.loop(1, DOMS)
        def _(k):
            dom = partner(k)
            send(
                fields_send.at[dom, b], fields_got.at[b, me],
                fields_ssem.at[b], fields_rsem.at[b], dom, my_bin,
            )

        fields_got[b, me] = fields_send[me, b]

    for n in range(ROWS):
        exit_field[:, n * LANES : (n + 1) * LANES] = field[n]

    sums[...] = jnp.zeros_like(sums)

    @pl.loop(0, BOUNCES)
    def _(b):
        await_bytes(fields_got.at[b, pl.ds(0, DOMS - 1)], fields_rsem.at[b])

        @pl.loop(0, DOMS // BATCH)
        def _(g):
            rows = [ids_got[g * BATCH + i, pl.ds(b, 1), :] for i in range(BATCH)]
            sums[...] += gathered_sums(rows, [fields_got[b, g * BATCH + i] for i in range(BATCH)])

    for k in range(1, BINS):
        other = (my_bin + k) % BINS
        send(
            sums.at[pl.ds(pl.multiple_of(other * 64, 64), 64)], sums_got.at[k - 1],
            sums_sems.at[0, k - 1], sums_sems.at[1, k - 1], me, other,
        )
    mine = sums[pl.ds(pl.multiple_of(my_bin * 64, 64), 64), :]
    fetch.wait()
    for k in range(1, BINS):
        await_bytes(sums_got.at[k - 1], sums_sems.at[1, k - 1])
        mine = mine + sums_got[k - 1]
    mine = mine.astype(BF16)

    width = 512
    is_real = iota((8, width), 0) < 4
    for at in range(0, 1024, width):
        real, imag = jnp.zeros((8, width), F32), jnp.zeros((8, width), F32)
        for hi in range(8):
            left = mine[8 * hi : 8 * hi + 8]
            lines = slice(256 * hi, 256 * (hi + 1))
            real = real + jnp.dot(left, held[0, lines, at : at + width], preferred_element_type=F32)
            imag = imag + jnp.dot(left, held[1, lines, at : at + width], preferred_element_type=F32)
        turned = pltpu.roll(imag, 4, 0)
        value = real + jnp.where(is_real, -turned, turned)
        for q in range(width // LANES):
            partial[at // LANES + q] = value[:, LANES * q : LANES * (q + 1)]

    @pl.loop(1, 8)
    def _(k):
        to = (z + k) % 8
        send(
            partial.at[to], along_got.at[z], along_sems.at[0], along_sems.at[1],
            to * 8 + me % 8, my_bin,
        )

    along_got[z] = partial[z]
    await_bytes(partial.at[pl.ds(0, 7)], along_sems.at[1])
    tile = along_got[0]
    for k in range(1, 8):
        tile = tile + along_got[k]
    piece[...] = tile
    spot = (me % 8) * BINS + my_bin

    @pl.loop(1, 32)
    def _(k):
        dom, bin_at = same_z(k)
        send(piece, last_got.at[spot], last_sems.at[0], last_sems.at[1], dom, bin_at)

    last_got[spot] = tile
    await_bytes(last_got.at[pl.ds(0, 31)], last_sems.at[1])
    tile = last_got[0]
    for k in range(1, 32):
        tile = tile + last_got[k]
    far[...] = tile

    await_bytes(ids_send.at[pl.ds(0, DOMS - 1)], ids_sems.at[0])
    for h in range(HALVES):
        await_bytes(facts_send.at[h, pl.ds(0, DOMS - 1)], facts_ssem.at[h])
    for b in range(BOUNCES):
        await_bytes(fields_got.at[b, pl.ds(0, DOMS - 1)], fields_ssem.at[b])
    for k in range(1, BINS):
        await_bytes(sums_got.at[k - 1], sums_sems.at[0, k - 1])
    await_bytes(partial.at[pl.ds(0, 7)], along_sems.at[0])
    await_bytes(last_got.at[pl.ds(0, 31)], last_sems.at[0])


def main(target, facet, table, phase, heading, field, weights):
    vmem = pltpu.VMEM
    dma = pltpu.SemaphoreType.DMA
    whole = pl.BlockSpec(memory_space=pltpu.VMEM)
    return pl.pallas_call(
        main_kernel,
        out_shape=(
            jax.ShapeDtypeStruct((8, LANES), F32),
            jax.ShapeDtypeStruct((8, ROWS * LANES), F32),
        ),
        in_specs=[whole] * 6 + [pl.BlockSpec(memory_space=pl.ANY)],
        out_specs=(whole, whole),
        scratch_shapes=[
            vmem((2, 2048, 1024), BF16),
            dma,
            vmem((DOMS, BOUNCES, CAP), I32),
            vmem((DOMS, BOUNCES, CAP), I32),
            vmem((BOUNCES, ROWS, LANES), I32),
            vmem((2 * 32 * PARAMS, 256), BF16),
            vmem((HALVES, DOMS, PARAMS, EACH, CAP), F32),
            vmem((HALVES, DOMS, PARAMS, EACH, CAP), F32),
            vmem((PARAMS, ROWS, LANES), F32),
            vmem((3, ROWS, LANES), F32),
            vmem((6, ROWS, LANES), F32),
            vmem((ROWS, 8, LANES), F32),
            vmem((DOMS, BOUNCES, 8, CAP), F32),
            vmem((BOUNCES, DOMS, 8, CAP), F32),
            vmem((256, 256), F32),
            vmem((BINS - 1, 64, 256), F32),
            vmem((8, 8, LANES), F32),
            vmem((8, 8, LANES), F32),
            vmem((8, LANES), F32),
            vmem((32, 8, LANES), F32),
            dma((2,)),
            dma((HALVES,)),
            dma((HALVES,)),
            dma((BOUNCES,)),
            dma((BOUNCES,)),
            dma((2, BINS - 1)),
            dma((2,)),
            dma((2,)),
        ],
        compiler_params=pltpu.CompilerParams(
            collective_id=0, has_side_effects=True, vmem_limit_bytes=48 << 20
        ),
    )(target, facet, table, phase, heading, field, weights)


def body(
    field_in,
    heading_in,
    launch_domain,
    hop_domain,
    hit_facet,
    path_phase,
    facet_polar,
    facet_azimuth,
    facet_tilt,
    surface_resistance,
    surface_reactance,
    kernel,
):
    grid = (ROWS, LANES)
    target = jnp.concatenate(
        [launch_domain.reshape(1, *grid), hop_domain.reshape(BOUNCES - 1, *grid)], axis=0
    )
    facet = hit_facet.reshape(BOUNCES, *grid)
    phase = path_phase.reshape(BOUNCES, *grid)
    heading = heading_in.reshape(3, *grid)
    table = jnp.concatenate(
        [
            p.reshape(32, 256)
            for p in (
                facet_polar, facet_azimuth, facet_tilt, surface_resistance, surface_reactance
            )
        ],
        axis=0,
    )
    far, exit_field = main(target, facet, table, phase, heading, field_in, kernel)
    spot = (lax.axis_index("dom") % 8) * BINS + lax.axis_index("bin")
    return lax.dynamic_slice_in_dim(far, spot * 4, 4, axis=1), exit_field


def solution(mesh):
    both = ("dom", "bin")
    in_specs = (
        P(None, both),
        P(None, both),
        P(both, None),
        P(None, both, None),
        P(None, both),
        P(None, both),
        P("dom"),
        P("dom"),
        P("dom"),
        P("dom"),
        P("dom"),
        P(None, both, None),
    )
    out_specs = (P(None, both), P(None, both))
    return jax.shard_map(body, mesh=mesh, in_specs=in_specs, out_specs=out_specs, check_vma=False)
```

```python
import jax
import jax.numpy as jnp
from jax import lax
from jax.experimental import pallas as pl
from jax.experimental.pallas import tpu as pltpu
from jax.sharding import PartitionSpec as P

BOUNCES = 4
HALVES = 2
EACH = BOUNCES // HALVES
DOMS = 64
BINS = 4
CAP = 128
LANES = 128
ROWS = 32
PARAMS = 5
BATCH = 16
F32 = jnp.float32
BF16 = jnp.bfloat16
I32 = jnp.int32
MESH = pl.DeviceIdType.MESH
LAST = (((1,), (1,)), ((), ()))


def iota(shape, dim):
    return lax.broadcasted_iota(I32, shape, dim)


def narrow(x):
    return x.astype(F32).astype(BF16)


def split(x):
    big = x.astype(BF16)
    return big, (x - big.astype(F32)).astype(BF16)


def one_hot(rows, depth):
    count = narrow(iota((depth, LANES), 0))
    one, zero = jnp.ones((depth, LANES), BF16), jnp.zeros((depth, LANES), BF16)
    hot = [jnp.where(count == narrow(jnp.broadcast_to(r, (depth, LANES))), one, zero) for r in rows]
    return jnp.concatenate(hot, axis=1)


def sin_cos(x):
    turns = jnp.floor(x * 0.6366197723675814 + 0.5)
    r = x - turns * 1.5703125
    r = r - turns * 4.83826794896e-4
    z = r * r
    s = ((-1.9515295891e-4 * z + 8.3321608736e-3) * z - 1.6666654611e-1) * z * r + r
    c = ((2.443315711809948e-5 * z - 1.388731625493765e-3) * z + 4.166664568298827e-2) * z * z
    c = c - 0.5 * z + 1.0
    odd = jnp.abs(turns) == 1.0
    near = turns == 0.0
    sine = jnp.where(odd, turns * c, jnp.where(near, s, -s))
    cosine = jnp.where(odd, -turns * s, jnp.where(near, c, -c))
    return sine, cosine


def divide(top_real, top_imag, low_real, low_imag):
    scale = 1.0 / (low_real * low_real + low_imag * low_imag)
    return (
        (top_real * low_real + top_imag * low_imag) * scale,
        (top_imag * low_real - top_real * low_imag) * scale,
    )


def lookup(table, rows, store):
    size = 32 * PARAMS
    found = jnp.dot(table[...], one_hot([r & 255 for r in rows], 256), preferred_element_type=F32)
    found = found[:size] + found[size:]
    for i, r in enumerate(rows):
        hi = jnp.broadcast_to(r >> 8, (8, LANES))
        group, line = hi >> 3, hi & 7
        for p in range(PARAMS):
            f = [
                found[32 * p + 8 * q : 32 * p + 8 * q + 8, LANES * i : LANES * (i + 1)]
                for q in range(4)
            ]
            y = jnp.where(
                group < 2, jnp.where(group == 0, f[0], f[1]), jnp.where(group == 2, f[2], f[3])
            )
            y = jnp.take_along_axis(y, line, axis=0, mode="promise_in_bounds")
            store(i, p, y[0:1])


def gathered_sums(rows, tiles):
    half = iota((16, LANES), 0) >> 3
    zero = jnp.zeros((16, LANES), BF16)
    parts = ([], [])
    for r, f in zip(rows, tiles):
        big = f.astype(BF16).astype(F32)
        hi = narrow(jnp.broadcast_to(r >> 8, (16, LANES)) - half)
        masks = [hi == jnp.asarray(2 * k, BF16) for k in range(16)]
        for part, value in zip(parts, (big, f - big)):
            twice = jnp.concatenate([value, value], axis=0).astype(BF16)
            part.append(jnp.concatenate([jnp.where(m, twice, zero) for m in masks], axis=0))
    left = jnp.concatenate([jnp.concatenate(part, axis=1) for part in parts], axis=0)
    total = lax.dot_general(
        left, one_hot([r & 255 for r in rows], 256), LAST, preferred_element_type=F32
    )
    return total[:256] + total[256:]


def ranks(b, target, facet, ids_out, slots):
    block = 2 * LANES
    blocks = ROWS // 2
    after = iota((block, 2 * block), 0) <= iota((block, 2 * block), 1)
    after = jnp.where(after | (iota((block, 2 * block), 1) >= block), 1.0, 0.0).astype(BF16)
    carry = jnp.zeros((DOMS, block), F32)
    doms = [target[b, n : n + 1, :] for n in range(ROWS)]
    marks = [one_hot(doms[2 * j : 2 * j + 2], DOMS) for j in range(blocks)]
    counts = jnp.dot(jnp.concatenate(marks, axis=0), after, preferred_element_type=F32)
    zero = jnp.zeros((DOMS, block), BF16)
    left, places = [], []
    for j in range(blocks):
        count = counts[DOMS * j : DOMS * (j + 1)]
        place = marks[j].astype(F32) * (count[:, :block] + carry)
        place = jnp.sum(place, axis=0, keepdims=True).astype(I32) - 1
        carry = carry + count[:, block:]
        for w in range(2):
            n = 2 * j + w
            mine = place[:, LANES * w : LANES * (w + 1)]
            slots[b, n : n + 1, :] = doms[n] * CAP + mine
            places.append(mine)
        ids = facet[pl.ds(b, 1), block * j : block * (j + 1)]
        left.append(
            jnp.concatenate(
                [
                    jnp.where(marks[j] > zero, narrow(jnp.broadcast_to(v, (DOMS, block))), zero)
                    for v in (ids >> 7, ids & 127)
                ],
                axis=0,
            )
        )
    packed = lax.dot_general(
        jnp.concatenate(left, axis=1), one_hot(places, CAP), LAST, preferred_element_type=F32
    ).astype(I32)
    row = packed[:DOMS]
    ids_out[:, b, :] = (row & 31) * 256 + (row >> 5) * 128 + packed[DOMS:]


def reflection(b, frame, phase, heading, coef):
    polar, azimuth, tilt, res, rea = (frame[p] for p in range(PARAMS))
    sin_p, cos_p = sin_cos(polar)
    sin_a, cos_a = sin_cos(azimuth)
    sin_t, cos_t = sin_cos(tilt)
    sin_f, cos_f = sin_cos(phase[b])
    normal = (sin_p * cos_a, sin_p * sin_a, cos_p)
    d = [heading[k] for k in range(3)]
    m = d[0] * normal[0] + d[1] * normal[1] + d[2] * normal[2]
    cosine = jnp.abs(m)
    te_r, te_i = divide(cosine - res, -rea, cosine + res, rea)
    rc, xc = res * cosine, rea * cosine
    tm_r, tm_i = divide(rc - 1.0, xc, rc + 1.0, xc)
    coef[0] = cos_t
    coef[1] = sin_t
    coef[2] = te_r * cos_f - te_i * sin_f
    coef[3] = te_r * sin_f + te_i * cos_f
    coef[4] = tm_r * cos_f - tm_i * sin_f
    coef[5] = tm_r * sin_f + tm_i * cos_f
    for k in range(3):
        heading[k] = d[k] - 2.0 * m * normal[k]


def reflect(coef, field):
    row = iota((8, LANES), 0)
    is_upper = (row & 2) == 0
    is_real = row < 4
    for n in range(ROWS):
        cos_t, sin_t, te_r, te_i, tm_r, tm_i = (
            jnp.broadcast_to(coef[k, n : n + 1, :], (8, LANES)) for k in range(6)
        )
        f = field[n]
        other = jnp.where(is_upper, pltpu.roll(f, 6, 0), -pltpu.roll(f, 2, 0))
        q = cos_t * f + sin_t * other
        turned = pltpu.roll(q, 4, 0)
        turned = jnp.where(is_real, -turned, turned)
        field[n] = jnp.where(is_upper, te_r, tm_r) * q + jnp.where(is_upper, te_i, tm_i) * turned


def main_kernel(
    launch_hbm, hops_hbm, facet_hbm, phase_hbm, heading_hbm, field_hbm,
    polar_hbm, azimuth_hbm, tilt_hbm, res_hbm, rea_hbm, weights,
    far, exit_field,
    held, target, facet, phase_in, heading_in, field_in, params,
    ids_send, ids_got, slots, rows_table,
    facts_send, facts_got, frame, phase, heading, coef, field,
    fields_send, fields_got, sums, sums_got, partial, along_got, piece, last_got,
    fetch_sems, ids_ssem, ids_rsem, facts_ssem, facts_rsem, fields_ssem, fields_rsem,
    sums_sems, along_sems, last_sems,
):
    me, my_bin = lax.axis_index("dom"), lax.axis_index("bin")
    z, y, core = me // 8, (me // 2) % 4, me % 2

    def partner(kz, q):
        return ((z + kz) % 8) * 8 + ((y + q // 2) % 4) * 2 + (core + q % 2) % 2

    def same_z(k):
        return partner(0, k % 8), (my_bin + k // 8) % BINS

    def near_first(i):
        return (8 + ((i + 1) // 2) * (2 * (i % 2) - 1)) % 8

    def send(source, landing, ssem, rsem, dom, bin_at):
        pltpu.make_async_remote_copy(
            src_ref=source, dst_ref=landing, send_sem=ssem, recv_sem=rsem,
            device_id=(dom, bin_at), device_id_type=MESH,
        ).start()

    def await_bytes(ref, sem):
        pltpu.make_async_copy(ref, ref, sem).wait()

    moves = [
        (launch_hbm, target.at[pl.ds(0, 1)]),
        (hops_hbm, target.at[pl.ds(1, BOUNCES - 1)]),
        (facet_hbm, facet),
        (polar_hbm, params.at[0]),
        (azimuth_hbm, params.at[1]),
        (tilt_hbm, params.at[2]),
        (res_hbm, params.at[3]),
        (rea_hbm, params.at[4]),
        (heading_hbm, heading_in),
        (phase_hbm, phase_in),
        (field_hbm, field_in),
        (weights, held),
    ]
    fetches = [
        pltpu.make_async_copy(source, landing, fetch_sems.at[i])
        for i, (source, landing) in enumerate(moves)
    ]
    for fetch in fetches:
        fetch.start()
    barrier = pltpu.get_barrier_semaphore()

    @pl.loop(1, DOMS)
    def _(k):
        dom = partner(k // 8, k % 8)
        pl.semaphore_signal(barrier, inc=1, device_id=(dom, my_bin), device_id_type=MESH)

    @pl.loop(8, 32)
    def _(k):
        pl.semaphore_signal(barrier, inc=1, device_id=same_z(k), device_id_type=MESH)

    for fetch in fetches[:3]:
        fetch.wait()

    @pl.loop(0, BOUNCES)
    def _(b):
        ranks(b, target, facet, ids_send, slots)

    pl.semaphore_wait(barrier, DOMS - 1 + 24)

    @pl.loop(0, DOMS)
    def _(k):
        kz = near_first(k // 8)
        dom = partner(kz, k % 8)

        @pl.when(k > 0)
        def _():
            send(ids_send.at[dom], ids_got.at[me], ids_ssem, ids_rsem.at[kz], dom, my_bin)

    ids_got[me] = ids_send[me]

    for fetch in fetches[3:11]:
        fetch.wait()
    for p in range(PARAMS):
        rows = jnp.concatenate([params[p, 0:32, :], params[p, 32:64, :]], axis=1)
        big, small = split(rows)
        rows_table[32 * p : 32 * (p + 1)] = big
        rows_table[32 * (PARAMS + p) : 32 * (PARAMS + p + 1)] = small
    for n in range(ROWS):
        lanes = slice(n * LANES, (n + 1) * LANES)
        heading[:, n, :] = heading_in[:, lanes]
        phase[:, n, :] = phase_in[:, lanes]
        field[n] = field_in[:, lanes]

    @pl.loop(0, HALVES)
    def _(h):
        @pl.loop(0, 8)
        def _(i):
            kz = near_first(i)
            first = ((z + 8 - kz) % 8) * 8

            @pl.when((h == 0) & (i == 0))
            def _():
                await_bytes(ids_send.at[pl.ds(0, 7)], ids_rsem.at[0])

            @pl.when((h == 0) & (i > 0))
            def _():
                await_bytes(ids_send.at[pl.ds(0, 8)], ids_rsem.at[kz])

            asked = [
                ids_got[first + q, pl.ds(EACH * h + w, 1), :] for q in range(8) for w in range(EACH)
            ]

            def store(n, p, value):
                facts_send[h, first + n // EACH, p, n % EACH : n % EACH + 1, :] = value

            lookup(rows_table, asked, store)

            @pl.loop(0, 8)
            def _(q):
                dom = partner(8 - kz, q)

                @pl.when((i > 0) | (q > 0))
                def _():
                    send(
                        facts_send.at[h, dom], facts_got.at[h, me],
                        facts_ssem.at[h], facts_rsem.at[h], dom, my_bin,
                    )

        facts_got[h, me] = facts_send[h, me]

    @pl.loop(0, BOUNCES)
    def _(b):
        h, w = b // EACH, b % EACH

        @pl.when(w == 0)
        def _():
            await_bytes(facts_send.at[h, pl.ds(0, DOMS - 1)], facts_rsem.at[h])

        for p in range(PARAMS):
            rows = [
                facts_got[h, pl.ds(j, 32, stride=2), p, pl.ds(w, 1), :].reshape(32, LANES)
                for j in range(2)
            ]
            big, small = split(jnp.concatenate(rows, axis=1))
            rows_table[32 * p : 32 * (p + 1)] = big
            rows_table[32 * (PARAMS + p) : 32 * (PARAMS + p + 1)] = small
        for part in range(ROWS // BATCH):

            def store(i, p, value, part=part):
                frame[p, part * BATCH + i : part * BATCH + i + 1, :] = value

            lookup(
                rows_table,
                [slots[b, n : n + 1, :] for n in range(part * BATCH, (part + 1) * BATCH)],
                store,
            )
        reflection(b, frame, phase, heading, coef)
        reflect(coef, field)
        total = None
        for part in range(ROWS // BATCH):
            lines = range(part * BATCH, (part + 1) * BATCH)
            more = gathered_sums([slots[b, n : n + 1, :] for n in lines], [field[n] for n in lines])
            total = more if total is None else total + more
        for hi in range(32):
            fields_send[2 * hi, b] = total[8 * hi : 8 * hi + 8, :LANES]
            fields_send[2 * hi + 1, b] = total[8 * hi : 8 * hi + 8, LANES:]

        @pl.loop(0, DOMS)
        def _(k):
            pair = k // 16
            kz = (1 - (k // 8) % 2) * (4 + pair) + ((k // 8) % 2) * (3 - pair)
            dom = partner(kz, k % 8)

            @pl.when((kz > 0) | (k % 8 > 0))
            def _():
                send(
                    fields_send.at[dom, b], fields_got.at[b, me],
                    fields_ssem.at[b], fields_rsem.at[b, pair], dom, my_bin,
                )

        fields_got[b, me] = fields_send[me, b]

    for n in range(ROWS):
        exit_field[:, n * LANES : (n + 1) * LANES] = field[n]

    sums[...] = jnp.zeros_like(sums)

    @pl.loop(0, BOUNCES)
    def _(b):
        @pl.loop(0, 4)
        def _(pair):
            @pl.when(pair < 3)
            def _():
                await_bytes(fields_got.at[b, pl.ds(0, 16)], fields_rsem.at[b, pair])

            @pl.when(pair == 3)
            def _():
                await_bytes(fields_got.at[b, pl.ds(0, 15)], fields_rsem.at[b, 3])

            firsts = [((z + 8 - kz) % 8) * 8 for kz in (4 + pair, 3 - pair)]
            senders = [first + q for first in firsts for q in range(8)]
            total = gathered_sums(
                [ids_got[dom, pl.ds(b, 1), :] for dom in senders],
                [fields_got[b, dom] for dom in senders],
            )
            for j in range(2):
                sums[j] += total[:, LANES * j : LANES * (j + 1)]

    for k in range(1, BINS):
        other = (my_bin + k) % BINS
        send(
            sums.at[other // 2, pl.ds(pl.multiple_of((other % 2) * 128, 128), 128)],
            sums_got.at[k - 1],
            sums_sems.at[0, k - 1], sums_sems.at[1, k - 1], me, other,
        )
    mine = sums[my_bin // 2, pl.ds(pl.multiple_of((my_bin % 2) * 128, 128), 128), :]
    fetches[11].wait()
    for k in range(1, BINS):
        await_bytes(sums_got.at[k - 1], sums_sems.at[1, k - 1])
        mine = mine + sums_got[k - 1]
    mine = mine.astype(BF16)

    width = 512
    is_real = iota((8, width), 0) < 4
    for at in range(0, 1024, width):
        real, imag = jnp.zeros((8, width), F32), jnp.zeros((8, width), F32)
        for hi in range(8):
            left = jnp.concatenate(
                [mine[16 * hi : 16 * hi + 8], mine[16 * hi + 8 : 16 * hi + 16]], axis=1
            )
            lines = slice(256 * hi, 256 * (hi + 1))
            real = real + jnp.dot(left, held[0, lines, at : at + width], preferred_element_type=F32)
            imag = imag + jnp.dot(left, held[1, lines, at : at + width], preferred_element_type=F32)
        turned = pltpu.roll(imag, 4, 0)
        value = real + jnp.where(is_real, -turned, turned)
        for q in range(width // LANES):
            partial[at // LANES + q] = value[:, LANES * q : LANES * (q + 1)]

    @pl.loop(1, 8)
    def _(k):
        to = (z + k) % 8
        send(
            partial.at[to], along_got.at[z], along_sems.at[0], along_sems.at[1],
            to * 8 + me % 8, my_bin,
        )

    along_got[z] = partial[z]
    await_bytes(partial.at[pl.ds(0, 7)], along_sems.at[1])
    tile = along_got[0]
    for k in range(1, 8):
        tile = tile + along_got[k]
    piece[...] = tile
    spot = (me % 8) * BINS + my_bin

    @pl.loop(1, 32)
    def _(k):
        dom, bin_at = same_z(k)
        send(piece, last_got.at[spot], last_sems.at[0], last_sems.at[1], dom, bin_at)

    last_got[spot] = tile
    await_bytes(last_got.at[pl.ds(0, 31)], last_sems.at[1])
    tile = last_got[0]
    for k in range(1, 32):
        tile = tile + last_got[k]
    far[...] = tile

    await_bytes(ids_send.at[pl.ds(0, DOMS - 1)], ids_ssem)
    for h in range(HALVES):
        await_bytes(facts_send.at[h, pl.ds(0, DOMS - 1)], facts_ssem.at[h])
    for b in range(BOUNCES):
        await_bytes(fields_got.at[b, pl.ds(0, DOMS - 1)], fields_ssem.at[b])
    for k in range(1, BINS):
        await_bytes(sums_got.at[k - 1], sums_sems.at[0, k - 1])
    await_bytes(partial.at[pl.ds(0, 7)], along_sems.at[0])
    await_bytes(last_got.at[pl.ds(0, 31)], last_sems.at[0])


def main(*args):
    vmem = pltpu.VMEM
    dma = pltpu.SemaphoreType.DMA
    whole = pl.BlockSpec(memory_space=pltpu.VMEM)
    return pl.pallas_call(
        main_kernel,
        out_shape=(
            jax.ShapeDtypeStruct((8, LANES), F32),
            jax.ShapeDtypeStruct((8, ROWS * LANES), F32),
        ),
        in_specs=[pl.BlockSpec(memory_space=pltpu.HBM)] * 12,
        out_specs=(whole, whole),
        scratch_shapes=[
            vmem((2, 2048, 1024), BF16),
            vmem((BOUNCES, ROWS, LANES), I32),
            vmem((BOUNCES, ROWS * LANES), I32),
            vmem((BOUNCES, ROWS * LANES), F32),
            vmem((3, ROWS * LANES), F32),
            vmem((8, ROWS * LANES), F32),
            vmem((PARAMS, 64, LANES), F32),
            vmem((DOMS, BOUNCES, CAP), I32),
            vmem((DOMS, BOUNCES, CAP), I32),
            vmem((BOUNCES, ROWS, LANES), I32),
            vmem((2 * 32 * PARAMS, 256), BF16),
            vmem((HALVES, DOMS, PARAMS, EACH, CAP), F32),
            vmem((HALVES, DOMS, PARAMS, EACH, CAP), F32),
            vmem((PARAMS, ROWS, LANES), F32),
            vmem((BOUNCES, ROWS, LANES), F32),
            vmem((3, ROWS, LANES), F32),
            vmem((6, ROWS, LANES), F32),
            vmem((ROWS, 8, LANES), F32),
            vmem((DOMS, BOUNCES, 8, CAP), F32),
            vmem((BOUNCES, DOMS, 8, CAP), F32),
            vmem((2, 256, LANES), F32),
            vmem((BINS - 1, 128, LANES), F32),
            vmem((8, 8, LANES), F32),
            vmem((8, 8, LANES), F32),
            vmem((8, LANES), F32),
            vmem((32, 8, LANES), F32),
            dma((12,)),
            dma,
            dma((8,)),
            dma((HALVES,)),
            dma((HALVES,)),
            dma((BOUNCES,)),
            dma((BOUNCES, 4)),
            dma((2, BINS - 1)),
            dma((2,)),
            dma((2,)),
        ],
        compiler_params=pltpu.CompilerParams(
            collective_id=0, has_side_effects=True, vmem_limit_bytes=67043328
        ),
    )(*args)


def body(
    field_in,
    heading_in,
    launch_domain,
    hop_domain,
    hit_facet,
    path_phase,
    facet_polar,
    facet_azimuth,
    facet_tilt,
    surface_resistance,
    surface_reactance,
    kernel,
):
    grid = (ROWS, LANES)
    params = (facet_polar, facet_azimuth, facet_tilt, surface_resistance, surface_reactance)
    far, exit_field = main(
        launch_domain.reshape(1, *grid),
        hop_domain.reshape(BOUNCES - 1, *grid),
        hit_facet,
        path_phase,
        heading_in,
        field_in,
        *(p.reshape(64, LANES) for p in params),
        kernel,
    )
    dom, bin_at = lax.axis_index("dom"), lax.axis_index("bin")
    spot = (dom % 8) * BINS + bin_at
    return lax.dynamic_slice_in_dim(far, spot * 4, 4, axis=1), exit_field


def solution(mesh):
    both = ("dom", "bin")
    in_specs = (
        P(None, both),
        P(None, both),
        P(both, None),
        P(None, both, None),
        P(None, both),
        P(None, both),
        P("dom"),
        P("dom"),
        P("dom"),
        P("dom"),
        P("dom"),
        P(None, both, None),
    )
    out_specs = (P(None, both), P(None, both))
    return jax.shard_map(body, mesh=mesh, in_specs=in_specs, out_specs=out_specs, check_vma=False)
```

```python
import jax
import jax.numpy as jnp
from jax import lax
from jax.experimental import pallas as pl
from jax.experimental.pallas import tpu as pltpu
from jax.sharding import PartitionSpec as P

BOUNCES = 4
HALVES = 2
EACH = BOUNCES // HALVES
DOMS = 64
BINS = 4
CAP = 128
LANES = 128
ROWS = 32
PARAMS = 5
BATCH = 16
F32 = jnp.float32
BF16 = jnp.bfloat16
I32 = jnp.int32
MESH = pl.DeviceIdType.MESH
LAST = (((1,), (1,)), ((), ()))


def iota(shape, dim):
    return lax.broadcasted_iota(I32, shape, dim)


def narrow(x):
    return x.astype(F32).astype(BF16)


def split(x):
    big = x.astype(BF16)
    return big, (x - big.astype(F32)).astype(BF16)


def one_hot(rows, depth):
    count = narrow(iota((depth, LANES), 0))
    one, zero = jnp.ones((depth, LANES), BF16), jnp.zeros((depth, LANES), BF16)
    hot = [jnp.where(count == narrow(jnp.broadcast_to(r, (depth, LANES))), one, zero) for r in rows]
    return jnp.concatenate(hot, axis=1)


def sin_cos(x):
    turns = jnp.floor(x * 0.6366197723675814 + 0.5)
    r = x - turns * 1.5703125
    r = r - turns * 4.83826794896e-4
    z = r * r
    s = ((-1.9515295891e-4 * z + 8.3321608736e-3) * z - 1.6666654611e-1) * z * r + r
    c = ((2.443315711809948e-5 * z - 1.388731625493765e-3) * z + 4.166664568298827e-2) * z * z
    c = c - 0.5 * z + 1.0
    odd = jnp.abs(turns) == 1.0
    near = turns == 0.0
    sine = jnp.where(odd, turns * c, jnp.where(near, s, -s))
    cosine = jnp.where(odd, -turns * s, jnp.where(near, c, -c))
    return sine, cosine


def divide(top_real, top_imag, low_real, low_imag):
    scale = 1.0 / (low_real * low_real + low_imag * low_imag)
    return (
        (top_real * low_real + top_imag * low_imag) * scale,
        (top_imag * low_real - top_real * low_imag) * scale,
    )


def lookup(table, rows, store):
    size = 32 * PARAMS
    found = jnp.dot(table[...], one_hot([r & 255 for r in rows], 256), preferred_element_type=F32)
    found = found[:size] + found[size:]
    for i, r in enumerate(rows):
        hi = jnp.broadcast_to(r >> 8, (8, LANES))
        group, line = hi >> 3, hi & 7
        for p in range(PARAMS):
            f = [
                found[32 * p + 8 * q : 32 * p + 8 * q + 8, LANES * i : LANES * (i + 1)]
                for q in range(4)
            ]
            y = jnp.where(
                group < 2, jnp.where(group == 0, f[0], f[1]), jnp.where(group == 2, f[2], f[3])
            )
            y = jnp.take_along_axis(y, line, axis=0, mode="promise_in_bounds")
            store(i, p, y[0:1])


def gathered_sums(rows, tiles):
    half = iota((16, LANES), 0) >> 3
    zero = jnp.zeros((16, LANES), BF16)
    parts = ([], [])
    for r, f in zip(rows, tiles):
        big = f.astype(BF16).astype(F32)
        hi = narrow(jnp.broadcast_to(r >> 8, (16, LANES)) - half)
        masks = [hi == jnp.asarray(2 * k, BF16) for k in range(16)]
        for part, value in zip(parts, (big, f - big)):
            twice = jnp.concatenate([value, value], axis=0).astype(BF16)
            part.append(jnp.concatenate([jnp.where(m, twice, zero) for m in masks], axis=0))
    left = jnp.concatenate([jnp.concatenate(part, axis=1) for part in parts], axis=0)
    total = lax.dot_general(
        left, one_hot([r & 255 for r in rows], 256), LAST, preferred_element_type=F32
    )
    return total[:256] + total[256:]


def ranks(b, target, facet, ids_out, slots):
    block = 2 * LANES
    blocks = ROWS // 2
    after = iota((block, 2 * block), 0) <= iota((block, 2 * block), 1)
    after = jnp.where(after | (iota((block, 2 * block), 1) >= block), 1.0, 0.0).astype(BF16)
    carry = jnp.zeros((DOMS, block), F32)
    doms = [target[b, n : n + 1, :] for n in range(ROWS)]
    marks = [one_hot(doms[2 * j : 2 * j + 2], DOMS) for j in range(blocks)]
    counts = jnp.dot(jnp.concatenate(marks, axis=0), after, preferred_element_type=F32)
    zero = jnp.zeros((DOMS, block), BF16)
    left, places = [], []
    for j in range(blocks):
        count = counts[DOMS * j : DOMS * (j + 1)]
        place = marks[j].astype(F32) * (count[:, :block] + carry)
        place = jnp.sum(place, axis=0, keepdims=True).astype(I32) - 1
        carry = carry + count[:, block:]
        for w in range(2):
            n = 2 * j + w
            mine = place[:, LANES * w : LANES * (w + 1)]
            slots[b, n : n + 1, :] = doms[n] * CAP + mine
            places.append(mine)
        ids = facet[pl.ds(b, 1), block * j : block * (j + 1)]
        left.append(
            jnp.concatenate(
                [
                    jnp.where(marks[j] > zero, narrow(jnp.broadcast_to(v, (DOMS, block))), zero)
                    for v in (ids >> 7, ids & 127)
                ],
                axis=0,
            )
        )
    packed = lax.dot_general(
        jnp.concatenate(left, axis=1), one_hot(places, CAP), LAST, preferred_element_type=F32
    ).astype(I32)
    row = packed[:DOMS]
    ids_out[:, b, :] = (row & 31) * 256 + (row >> 5) * 128 + packed[DOMS:]


def reflection(b, frame, phase, heading, coef):
    polar, azimuth, tilt, res, rea = (frame[p] for p in range(PARAMS))
    sin_p, cos_p = sin_cos(polar)
    sin_a, cos_a = sin_cos(azimuth)
    sin_t, cos_t = sin_cos(tilt)
    sin_f, cos_f = sin_cos(phase[b])
    normal = (sin_p * cos_a, sin_p * sin_a, cos_p)
    d = [heading[k] for k in range(3)]
    m = d[0] * normal[0] + d[1] * normal[1] + d[2] * normal[2]
    cosine = jnp.abs(m)
    te_r, te_i = divide(cosine - res, -rea, cosine + res, rea)
    rc, xc = res * cosine, rea * cosine
    tm_r, tm_i = divide(rc - 1.0, xc, rc + 1.0, xc)
    coef[0] = cos_t
    coef[1] = sin_t
    coef[2] = te_r * cos_f - te_i * sin_f
    coef[3] = te_r * sin_f + te_i * cos_f
    coef[4] = tm_r * cos_f - tm_i * sin_f
    coef[5] = tm_r * sin_f + tm_i * cos_f
    for k in range(3):
        heading[k] = d[k] - 2.0 * m * normal[k]


def reflect(coef, field):
    row = iota((8, LANES), 0)
    is_upper = (row & 2) == 0
    is_real = row < 4
    for n in range(ROWS):
        cos_t, sin_t, te_r, te_i, tm_r, tm_i = (
            jnp.broadcast_to(coef[k, n : n + 1, :], (8, LANES)) for k in range(6)
        )
        f = field[n]
        other = jnp.where(is_upper, pltpu.roll(f, 6, 0), -pltpu.roll(f, 2, 0))
        q = cos_t * f + sin_t * other
        turned = pltpu.roll(q, 4, 0)
        turned = jnp.where(is_real, -turned, turned)
        field[n] = jnp.where(is_upper, te_r, tm_r) * q + jnp.where(is_upper, te_i, tm_i) * turned


def main_kernel(
    launch_hbm, hops_hbm, facet_hbm, phase_hbm, heading_hbm, field_hbm,
    polar_hbm, azimuth_hbm, tilt_hbm, res_hbm, rea_hbm, weights,
    far, exit_field,
    held, target, facet, phase_in, heading_in, field_in, params,
    ids_send, ids_got, slots, rows_table,
    facts_send, facts_got, frame, phase, heading, coef, field,
    fields_send, fields_got, sums, sums_got, partial, along_got, piece, last_got,
    fetch_sems, ids_ssem, ids_rsem, facts_ssem, facts_rsem, fields_ssem, fields_rsem,
    sums_sems, along_sems, last_sems,
):
    me, my_bin = lax.axis_index("dom"), lax.axis_index("bin")
    z, y, core = me // 8, (me // 2) % 4, me % 2

    def partner(kz, q):
        return ((z + kz) % 8) * 8 + ((y + q // 2) % 4) * 2 + (core + q % 2) % 2

    def same_z(k):
        return partner(0, k % 8), (my_bin + k // 8) % BINS

    def near_first(i):
        return (8 + ((i + 1) // 2) * (2 * (i % 2) - 1)) % 8

    def send(source, landing, ssem, rsem, dom, bin_at):
        pltpu.make_async_remote_copy(
            src_ref=source, dst_ref=landing, send_sem=ssem, recv_sem=rsem,
            device_id=(dom, bin_at), device_id_type=MESH,
        ).start()

    def await_bytes(ref, sem):
        pltpu.make_async_copy(ref, ref, sem).wait()

    moves = [
        (launch_hbm, target.at[pl.ds(0, 1)]),
        (hops_hbm, target.at[pl.ds(1, BOUNCES - 1)]),
        (facet_hbm, facet),
        (polar_hbm, params.at[0]),
        (azimuth_hbm, params.at[1]),
        (tilt_hbm, params.at[2]),
        (res_hbm, params.at[3]),
        (rea_hbm, params.at[4]),
        (heading_hbm, heading_in),
        (phase_hbm, phase_in),
        (field_hbm, field_in),
        (weights, held),
    ]
    fetches = [
        pltpu.make_async_copy(source, landing, fetch_sems.at[i])
        for i, (source, landing) in enumerate(moves)
    ]
    for fetch in fetches:
        fetch.start()
    barrier = pltpu.get_barrier_semaphore()

    @pl.loop(1, DOMS)
    def _(k):
        dom = partner(k // 8, k % 8)
        pl.semaphore_signal(barrier, inc=1, device_id=(dom, my_bin), device_id_type=MESH)

    @pl.loop(8, 32)
    def _(k):
        pl.semaphore_signal(barrier, inc=1, device_id=same_z(k), device_id_type=MESH)

    for fetch in fetches[:3]:
        fetch.wait()

    @pl.loop(0, BOUNCES)
    def _(b):
        ranks(b, target, facet, ids_send, slots)

    pl.semaphore_wait(barrier, DOMS - 1 + 24)

    @pl.loop(0, DOMS)
    def _(k):
        kz = near_first(k // 8)
        dom = partner(kz, k % 8)

        @pl.when(k > 0)
        def _():
            send(ids_send.at[dom], ids_got.at[me], ids_ssem, ids_rsem.at[kz], dom, my_bin)

    ids_got[me] = ids_send[me]

    for fetch in fetches[3:11]:
        fetch.wait()
    for p in range(PARAMS):
        rows = jnp.concatenate([params[p, 0:32, :], params[p, 32:64, :]], axis=1)
        big, small = split(rows)
        rows_table[32 * p : 32 * (p + 1)] = big
        rows_table[32 * (PARAMS + p) : 32 * (PARAMS + p + 1)] = small
    for n in range(ROWS):
        lanes = slice(n * LANES, (n + 1) * LANES)
        heading[:, n, :] = heading_in[:, lanes]
        phase[:, n, :] = phase_in[:, lanes]
        field[n] = field_in[:, lanes]

    @pl.loop(0, HALVES)
    def _(h):
        @pl.loop(0, 8)
        def _(i):
            kz = near_first(i)
            first = ((z + 8 - kz) % 8) * 8

            @pl.when((h == 0) & (i == 0))
            def _():
                await_bytes(ids_send.at[pl.ds(0, 7)], ids_rsem.at[0])

            @pl.when((h == 0) & (i > 0))
            def _():
                await_bytes(ids_send.at[pl.ds(0, 8)], ids_rsem.at[kz])

            asked = [
                ids_got[first + q, pl.ds(EACH * h + w, 1), :] for q in range(8) for w in range(EACH)
            ]

            def store(n, p, value):
                facts_send[h, first + n // EACH, p, n % EACH : n % EACH + 1, :] = value

            lookup(rows_table, asked, store)

            @pl.loop(0, 8)
            def _(q):
                dom = partner(8 - kz, q)

                @pl.when((i > 0) | (q > 0))
                def _():
                    send(
                        facts_send.at[h, dom], facts_got.at[h, me],
                        facts_ssem.at[h], facts_rsem.at[h], dom, my_bin,
                    )

        facts_got[h, me] = facts_send[h, me]

    @pl.loop(0, BOUNCES)
    def _(b):
        h, w = b // EACH, b % EACH

        @pl.when(w == 0)
        def _():
            await_bytes(facts_send.at[h, pl.ds(0, DOMS - 1)], facts_rsem.at[h])

        for p in range(PARAMS):
            rows = [
                facts_got[h, pl.ds(j, 32, stride=2), p, pl.ds(w, 1), :].reshape(32, LANES)
                for j in range(2)
            ]
            big, small = split(jnp.concatenate(rows, axis=1))
            rows_table[32 * p : 32 * (p + 1)] = big
            rows_table[32 * (PARAMS + p) : 32 * (PARAMS + p + 1)] = small
        for part in range(ROWS // BATCH):

            def store(i, p, value, part=part):
                frame[p, part * BATCH + i : part * BATCH + i + 1, :] = value

            lookup(
                rows_table,
                [slots[b, n : n + 1, :] for n in range(part * BATCH, (part + 1) * BATCH)],
                store,
            )
        reflection(b, frame, phase, heading, coef)
        reflect(coef, field)
        total = None
        for part in range(ROWS // BATCH):
            lines = range(part * BATCH, (part + 1) * BATCH)
            more = gathered_sums([slots[b, n : n + 1, :] for n in lines], [field[n] for n in lines])
            total = more if total is None else total + more
        for hi in range(32):
            fields_send[2 * hi, b] = total[8 * hi : 8 * hi + 8, :LANES]
            fields_send[2 * hi + 1, b] = total[8 * hi : 8 * hi + 8, LANES:]

        @pl.loop(0, DOMS)
        def _(k):
            pair = k // 16
            kz = (1 - (k // 8) % 2) * (4 + pair) + ((k // 8) % 2) * (3 - pair)
            dom = partner(kz, k % 8)

            @pl.when((kz > 0) | (k % 8 > 0))
            def _():
                send(
                    fields_send.at[dom, b], fields_got.at[b, me],
                    fields_ssem.at[b], fields_rsem.at[b, pair], dom, my_bin,
                )

        fields_got[b, me] = fields_send[me, b]

    for n in range(ROWS):
        exit_field[:, n * LANES : (n + 1) * LANES] = field[n]

    sums[...] = jnp.zeros_like(sums)

    @pl.loop(0, BOUNCES)
    def _(b):
        @pl.loop(0, 4)
        def _(pair):
            @pl.when(pair < 3)
            def _():
                await_bytes(fields_got.at[b, pl.ds(0, 16)], fields_rsem.at[b, pair])

            @pl.when(pair == 3)
            def _():
                await_bytes(fields_got.at[b, pl.ds(0, 15)], fields_rsem.at[b, 3])

            firsts = [((z + 8 - kz) % 8) * 8 for kz in (4 + pair, 3 - pair)]
            senders = [first + q for first in firsts for q in range(8)]
            total = gathered_sums(
                [ids_got[dom, pl.ds(b, 1), :] for dom in senders],
                [fields_got[b, dom] for dom in senders],
            )
            for j in range(2):
                sums[j] += total[:, LANES * j : LANES * (j + 1)]

    for k in range(1, BINS):
        other = (my_bin + k) % BINS
        send(
            sums.at[other // 2, pl.ds(pl.multiple_of((other % 2) * 128, 128), 128)],
            sums_got.at[k - 1],
            sums_sems.at[0, k - 1], sums_sems.at[1, k - 1], me, other,
        )
    mine = sums[my_bin // 2, pl.ds(pl.multiple_of((my_bin % 2) * 128, 128), 128), :]
    fetches[11].wait()
    for k in range(1, BINS):
        await_bytes(sums_got.at[k - 1], sums_sems.at[1, k - 1])
        mine = mine + sums_got[k - 1]
    mine = mine.astype(BF16)

    width = 512
    is_real = iota((8, width), 0) < 4
    for at in range(0, 1024, width):
        real, imag = jnp.zeros((8, width), F32), jnp.zeros((8, width), F32)
        for hi in range(8):
            left = jnp.concatenate(
                [mine[16 * hi : 16 * hi + 8], mine[16 * hi + 8 : 16 * hi + 16]], axis=1
            )
            lines = slice(256 * hi, 256 * (hi + 1))
            real = real + jnp.dot(left, held[0, lines, at : at + width], preferred_element_type=F32)
            imag = imag + jnp.dot(left, held[1, lines, at : at + width], preferred_element_type=F32)
        turned = pltpu.roll(imag, 4, 0)
        value = real + jnp.where(is_real, -turned, turned)
        for q in range(width // LANES):
            partial[at // LANES + q] = value[:, LANES * q : LANES * (q + 1)]

    @pl.loop(1, 8)
    def _(k):
        to = (z + k) % 8
        send(
            partial.at[to], along_got.at[z], along_sems.at[0], along_sems.at[1],
            to * 8 + me % 8, my_bin,
        )

    along_got[z] = partial[z]
    await_bytes(partial.at[pl.ds(0, 7)], along_sems.at[1])
    tile = along_got[0]
    for k in range(1, 8):
        tile = tile + along_got[k]
    piece[...] = tile
    spot = (me % 8) * BINS + my_bin

    @pl.loop(1, 32)
    def _(k):
        dom, bin_at = same_z(k)
        send(piece, last_got.at[spot], last_sems.at[0], last_sems.at[1], dom, bin_at)

    last_got[spot] = tile
    await_bytes(last_got.at[pl.ds(0, 31)], last_sems.at[1])
    tile = last_got[0]
    for k in range(1, 32):
        tile = tile + last_got[k]
    far[...] = tile

    await_bytes(ids_send.at[pl.ds(0, DOMS - 1)], ids_ssem)
    for h in range(HALVES):
        await_bytes(facts_send.at[h, pl.ds(0, DOMS - 1)], facts_ssem.at[h])
    for b in range(BOUNCES):
        await_bytes(fields_got.at[b, pl.ds(0, DOMS - 1)], fields_ssem.at[b])
    for k in range(1, BINS):
        await_bytes(sums_got.at[k - 1], sums_sems.at[0, k - 1])
    await_bytes(partial.at[pl.ds(0, 7)], along_sems.at[0])
    await_bytes(last_got.at[pl.ds(0, 31)], last_sems.at[0])


def main(*args):
    vmem = pltpu.VMEM
    dma = pltpu.SemaphoreType.DMA
    whole = pl.BlockSpec(memory_space=pltpu.VMEM)
    return pl.pallas_call(
        main_kernel,
        out_shape=(
            jax.ShapeDtypeStruct((8, LANES), F32),
            jax.ShapeDtypeStruct((8, ROWS * LANES), F32),
        ),
        in_specs=[pl.BlockSpec(memory_space=pltpu.HBM)] * 12,
        out_specs=(whole, whole),
        scratch_shapes=[
            vmem((2, 2048, 1024), BF16),
            vmem((BOUNCES, ROWS, LANES), I32),
            vmem((BOUNCES, ROWS * LANES), I32),
            vmem((BOUNCES, ROWS * LANES), F32),
            vmem((3, ROWS * LANES), F32),
            vmem((8, ROWS * LANES), F32),
            vmem((PARAMS, 64, LANES), F32),
            vmem((DOMS, BOUNCES, CAP), I32),
            vmem((DOMS, BOUNCES, CAP), I32),
            vmem((BOUNCES, ROWS, LANES), I32),
            vmem((2 * 32 * PARAMS, 256), BF16),
            vmem((HALVES, DOMS, PARAMS, EACH, CAP), F32),
            vmem((HALVES, DOMS, PARAMS, EACH, CAP), F32),
            vmem((PARAMS, ROWS, LANES), F32),
            vmem((BOUNCES, ROWS, LANES), F32),
            vmem((3, ROWS, LANES), F32),
            vmem((6, ROWS, LANES), F32),
            vmem((ROWS, 8, LANES), F32),
            vmem((DOMS, BOUNCES, 8, CAP), F32),
            vmem((BOUNCES, DOMS, 8, CAP), F32),
            vmem((2, 256, LANES), F32),
            vmem((BINS - 1, 128, LANES), F32),
            vmem((8, 8, LANES), F32),
            vmem((8, 8, LANES), F32),
            vmem((8, LANES), F32),
            vmem((32, 8, LANES), F32),
            dma((12,)),
            dma,
            dma((8,)),
            dma((HALVES,)),
            dma((HALVES,)),
            dma((BOUNCES,)),
            dma((BOUNCES, 4)),
            dma((2, BINS - 1)),
            dma((2,)),
            dma((2,)),
        ],
        compiler_params=pltpu.CompilerParams(
            collective_id=0, has_side_effects=True, vmem_limit_bytes=48 << 20
        ),
    )(*(pltpu.with_memory_space_constraint(a, pltpu.HBM) for a in args))


def body(
    field_in,
    heading_in,
    launch_domain,
    hop_domain,
    hit_facet,
    path_phase,
    facet_polar,
    facet_azimuth,
    facet_tilt,
    surface_resistance,
    surface_reactance,
    kernel,
):
    grid = (ROWS, LANES)
    params = (facet_polar, facet_azimuth, facet_tilt, surface_resistance, surface_reactance)
    far, exit_field = main(
        launch_domain.reshape(1, *grid),
        hop_domain.reshape(BOUNCES - 1, *grid),
        hit_facet,
        path_phase,
        heading_in,
        field_in,
        *(p.reshape(64, LANES) for p in params),
        kernel,
    )
    dom, bin_at = lax.axis_index("dom"), lax.axis_index("bin")
    spot = (dom % 8) * BINS + bin_at
    return lax.dynamic_slice_in_dim(far, spot * 4, 4, axis=1), exit_field


def solution(mesh):
    both = ("dom", "bin")
    in_specs = (
        P(None, both),
        P(None, both),
        P(both, None),
        P(None, both, None),
        P(None, both),
        P(None, both),
        P("dom"),
        P("dom"),
        P("dom"),
        P("dom"),
        P("dom"),
        P(None, both, None),
    )
    out_specs = (P(None, both), P(None, both))
    return jax.shard_map(body, mesh=mesh, in_specs=in_specs, out_specs=out_specs, check_vma=False)
```

```python
import jax
import jax.numpy as jnp
from jax import lax
from jax.experimental import pallas as pl
from jax.experimental.pallas import tpu as pltpu
from jax.sharding import PartitionSpec as P

BOUNCES = 4
HALVES = 2
EACH = BOUNCES // HALVES
DOMS = 64
BINS = 4
CAP = 128
LANES = 128
ROWS = 32
PARAMS = 5
BATCH = 16
F32 = jnp.float32
BF16 = jnp.bfloat16
I32 = jnp.int32
MESH = pl.DeviceIdType.MESH
LAST = (((1,), (1,)), ((), ()))


def iota(shape, dim):
    return lax.broadcasted_iota(I32, shape, dim)


def narrow(x):
    return x.astype(F32).astype(BF16)


def split(x):
    big = x.astype(BF16)
    return big, (x - big.astype(F32)).astype(BF16)


def one_hot(rows, depth):
    count = narrow(iota((depth, LANES), 0))
    one, zero = jnp.ones((depth, LANES), BF16), jnp.zeros((depth, LANES), BF16)
    hot = [jnp.where(count == narrow(jnp.broadcast_to(r, (depth, LANES))), one, zero) for r in rows]
    return jnp.concatenate(hot, axis=1)


def sin_cos(x):
    turns = jnp.floor(x * 0.6366197723675814 + 0.5)
    r = x - turns * 1.5703125
    r = r - turns * 4.83826794896e-4
    z = r * r
    s = ((-1.9515295891e-4 * z + 8.3321608736e-3) * z - 1.6666654611e-1) * z * r + r
    c = ((2.443315711809948e-5 * z - 1.388731625493765e-3) * z + 4.166664568298827e-2) * z * z
    c = c - 0.5 * z + 1.0
    odd = jnp.abs(turns) == 1.0
    near = turns == 0.0
    sine = jnp.where(odd, turns * c, jnp.where(near, s, -s))
    cosine = jnp.where(odd, -turns * s, jnp.where(near, c, -c))
    return sine, cosine


def divide(top_real, top_imag, low_real, low_imag):
    scale = 1.0 / (low_real * low_real + low_imag * low_imag)
    return (
        (top_real * low_real + top_imag * low_imag) * scale,
        (top_imag * low_real - top_real * low_imag) * scale,
    )


def lookup(table, rows, store):
    size = 32 * PARAMS
    found = jnp.dot(table[...], one_hot([r & 255 for r in rows], 256), preferred_element_type=F32)
    found = found[:size] + found[size:]
    for i, r in enumerate(rows):
        hi = jnp.broadcast_to(r >> 8, (8, LANES))
        group, line = hi >> 3, hi & 7
        for p in range(PARAMS):
            f = [
                found[32 * p + 8 * q : 32 * p + 8 * q + 8, LANES * i : LANES * (i + 1)]
                for q in range(4)
            ]
            y = jnp.where(
                group < 2, jnp.where(group == 0, f[0], f[1]), jnp.where(group == 2, f[2], f[3])
            )
            y = jnp.take_along_axis(y, line, axis=0, mode="promise_in_bounds")
            store(i, p, y[0:1])


def gathered_sums(rows, tiles):
    half = iota((16, LANES), 0) >> 3
    zero = jnp.zeros((16, LANES), BF16)
    parts = ([], [])
    for r, f in zip(rows, tiles):
        big = f.astype(BF16).astype(F32)
        hi = narrow(jnp.broadcast_to(r >> 8, (16, LANES)) - half)
        masks = [hi == jnp.asarray(2 * k, BF16) for k in range(16)]
        for part, value in zip(parts, (big, f - big)):
            twice = jnp.concatenate([value, value], axis=0).astype(BF16)
            part.append(jnp.concatenate([jnp.where(m, twice, zero) for m in masks], axis=0))
    left = jnp.concatenate([jnp.concatenate(part, axis=1) for part in parts], axis=0)
    total = lax.dot_general(
        left, one_hot([r & 255 for r in rows], 256), LAST, preferred_element_type=F32
    )
    return total[:256] + total[256:]


def ranks(b, target, facet, ids_out, slots):
    block = 2 * LANES
    blocks = ROWS // 2
    after = iota((block, 2 * block), 0) <= iota((block, 2 * block), 1)
    after = jnp.where(after | (iota((block, 2 * block), 1) >= block), 1.0, 0.0).astype(BF16)
    carry = jnp.zeros((DOMS, block), F32)
    doms = [target[b, n : n + 1, :] for n in range(ROWS)]
    marks = [one_hot(doms[2 * j : 2 * j + 2], DOMS) for j in range(blocks)]
    counts = jnp.dot(jnp.concatenate(marks, axis=0), after, preferred_element_type=F32)
    zero = jnp.zeros((DOMS, block), BF16)
    left, places = [], []
    for j in range(blocks):
        count = counts[DOMS * j : DOMS * (j + 1)]
        place = marks[j].astype(F32) * (count[:, :block] + carry)
        place = jnp.sum(place, axis=0, keepdims=True).astype(I32) - 1
        carry = carry + count[:, block:]
        for w in range(2):
            n = 2 * j + w
            mine = place[:, LANES * w : LANES * (w + 1)]
            slots[b, n : n + 1, :] = doms[n] * CAP + mine
            places.append(mine)
        ids = facet[pl.ds(b, 1), block * j : block * (j + 1)]
        left.append(
            jnp.concatenate(
                [
                    jnp.where(marks[j] > zero, narrow(jnp.broadcast_to(v, (DOMS, block))), zero)
                    for v in (ids >> 7, ids & 127)
                ],
                axis=0,
            )
        )
    packed = lax.dot_general(
        jnp.concatenate(left, axis=1), one_hot(places, CAP), LAST, preferred_element_type=F32
    ).astype(I32)
    row = packed[:DOMS]
    ids_out[:, b, :] = (row & 31) * 256 + (row >> 5) * 128 + packed[DOMS:]


def reflection(b, frame, phase, heading, coef):
    polar, azimuth, tilt, res, rea = (frame[p] for p in range(PARAMS))
    sin_p, cos_p = sin_cos(polar)
    sin_a, cos_a = sin_cos(azimuth)
    sin_t, cos_t = sin_cos(tilt)
    sin_f, cos_f = sin_cos(phase[b])
    normal = (sin_p * cos_a, sin_p * sin_a, cos_p)
    d = [heading[k] for k in range(3)]
    m = d[0] * normal[0] + d[1] * normal[1] + d[2] * normal[2]
    cosine = jnp.abs(m)
    te_r, te_i = divide(cosine - res, -rea, cosine + res, rea)
    rc, xc = res * cosine, rea * cosine
    tm_r, tm_i = divide(rc - 1.0, xc, rc + 1.0, xc)
    coef[0] = cos_t
    coef[1] = sin_t
    coef[2] = te_r * cos_f - te_i * sin_f
    coef[3] = te_r * sin_f + te_i * cos_f
    coef[4] = tm_r * cos_f - tm_i * sin_f
    coef[5] = tm_r * sin_f + tm_i * cos_f
    for k in range(3):
        heading[k] = d[k] - 2.0 * m * normal[k]


def reflect(coef, field):
    row = iota((8, LANES), 0)
    is_upper = (row & 2) == 0
    is_real = row < 4
    for n in range(ROWS):
        cos_t, sin_t, te_r, te_i, tm_r, tm_i = (
            jnp.broadcast_to(coef[k, n : n + 1, :], (8, LANES)) for k in range(6)
        )
        f = field[n]
        other = jnp.where(is_upper, pltpu.roll(f, 6, 0), -pltpu.roll(f, 2, 0))
        q = cos_t * f + sin_t * other
        turned = pltpu.roll(q, 4, 0)
        turned = jnp.where(is_real, -turned, turned)
        field[n] = jnp.where(is_upper, te_r, tm_r) * q + jnp.where(is_upper, te_i, tm_i) * turned


def main_kernel(
    launch_hbm, hops_hbm, facet_hbm, phase_hbm, heading_hbm, field_hbm,
    polar_hbm, azimuth_hbm, tilt_hbm, res_hbm, rea_hbm, weights,
    far, exit_field,
    held, target, facet, phase_in, heading_in, field_in, params,
    ids_send, ids_got, slots, rows_table,
    facts_send, facts_got, frame, phase, heading, coef, field,
    fields_send, fields_got, sums, sums_got, partial, along_got, piece, last_got,
    fetch_sems, ids_ssem, ids_rsem, facts_ssem, facts_rsem, fields_ssem, fields_rsem,
    sums_sems, along_sems, last_sems,
):
    me, my_bin = lax.axis_index("dom"), lax.axis_index("bin")
    z, y, core = me // 8, (me // 2) % 4, me % 2

    places = [((y + q // 2) % 4) * 2 + (core + q % 2) % 2 for q in range(8)]

    def each_of_plane(plane, skip_first, action):
        for q in range(8):
            if q == 0:
                pl.when(jnp.logical_not(skip_first))(lambda: action(plane * 8 + places[0]))
            else:
                action(plane * 8 + places[q])

    def partner(kz, q):
        return ((z + kz) % 8) * 8 + ((y + q // 2) % 4) * 2 + (core + q % 2) % 2

    def same_z(k):
        return partner(0, k % 8), (my_bin + k // 8) % BINS

    def near_first(i):
        return (8 + ((i + 1) // 2) * (2 * (i % 2) - 1)) % 8

    def send(source, landing, ssem, rsem, dom, bin_at):
        pltpu.make_async_remote_copy(
            src_ref=source, dst_ref=landing, send_sem=ssem, recv_sem=rsem,
            device_id=(dom, bin_at), device_id_type=MESH,
        ).start()

    def await_bytes(ref, sem):
        pltpu.make_async_copy(ref, ref, sem).wait()

    moves = [
        (launch_hbm, target.at[pl.ds(0, 1)]),
        (hops_hbm, target.at[pl.ds(1, BOUNCES - 1)]),
        (facet_hbm, facet),
        (polar_hbm, params.at[0]),
        (azimuth_hbm, params.at[1]),
        (tilt_hbm, params.at[2]),
        (res_hbm, params.at[3]),
        (rea_hbm, params.at[4]),
        (heading_hbm, heading_in),
        (phase_hbm, phase_in),
        (field_hbm, field_in),
        (weights, held),
    ]
    fetches = [
        pltpu.make_async_copy(source, landing, fetch_sems.at[i])
        for i, (source, landing) in enumerate(moves)
    ]
    for fetch in fetches:
        fetch.start()
    barrier = pltpu.get_barrier_semaphore()

    @pl.loop(0, 8)
    def _(kz):
        def greet(dom):
            pl.semaphore_signal(barrier, inc=1, device_id=(dom, my_bin), device_id_type=MESH)

        each_of_plane((z + kz) % 8, kz == 0, greet)

    @pl.loop(8, 32)
    def _(k):
        pl.semaphore_signal(barrier, inc=1, device_id=same_z(k), device_id_type=MESH)

    for fetch in fetches[:3]:
        fetch.wait()

    @pl.loop(0, BOUNCES)
    def _(b):
        ranks(b, target, facet, ids_send, slots)

    pl.semaphore_wait(barrier, DOMS - 1 + 24)

    @pl.loop(0, 8)
    def _(i):
        kz = near_first(i)

        def ask(dom):
            send(ids_send.at[dom], ids_got.at[me], ids_ssem, ids_rsem.at[kz], dom, my_bin)

        each_of_plane((z + kz) % 8, i == 0, ask)

    ids_got[me] = ids_send[me]

    for fetch in fetches[3:11]:
        fetch.wait()
    for p in range(PARAMS):
        rows = jnp.concatenate([params[p, 0:32, :], params[p, 32:64, :]], axis=1)
        big, small = split(rows)
        rows_table[32 * p : 32 * (p + 1)] = big
        rows_table[32 * (PARAMS + p) : 32 * (PARAMS + p + 1)] = small
    for n in range(ROWS):
        lanes = slice(n * LANES, (n + 1) * LANES)
        heading[:, n, :] = heading_in[:, lanes]
        phase[:, n, :] = phase_in[:, lanes]
        field[n] = field_in[:, lanes]

    @pl.loop(0, HALVES)
    def _(h):
        @pl.loop(0, 8)
        def _(i):
            kz = near_first(i)
            first = ((z + 8 - kz) % 8) * 8

            @pl.when((h == 0) & (i == 0))
            def _():
                await_bytes(ids_send.at[pl.ds(0, 7)], ids_rsem.at[0])

            @pl.when((h == 0) & (i > 0))
            def _():
                await_bytes(ids_send.at[pl.ds(0, 8)], ids_rsem.at[kz])

            asked = [
                ids_got[first + q, pl.ds(EACH * h + w, 1), :] for q in range(8) for w in range(EACH)
            ]

            def store(n, p, value):
                facts_send[h, first + n // EACH, p, n % EACH : n % EACH + 1, :] = value

            lookup(rows_table, asked, store)

            def answer(dom):
                send(
                    facts_send.at[h, dom], facts_got.at[h, me],
                    facts_ssem.at[h], facts_rsem.at[h], dom, my_bin,
                )

            each_of_plane((z + 8 - kz) % 8, i == 0, answer)

        facts_got[h, me] = facts_send[h, me]

    @pl.loop(0, BOUNCES)
    def _(b):
        h, w = b // EACH, b % EACH

        @pl.when(w == 0)
        def _():
            await_bytes(facts_send.at[h, pl.ds(0, DOMS - 1)], facts_rsem.at[h])

        for p in range(PARAMS):
            rows = [
                facts_got[h, pl.ds(j, 32, stride=2), p, pl.ds(w, 1), :].reshape(32, LANES)
                for j in range(2)
            ]
            big, small = split(jnp.concatenate(rows, axis=1))
            rows_table[32 * p : 32 * (p + 1)] = big
            rows_table[32 * (PARAMS + p) : 32 * (PARAMS + p + 1)] = small
        for part in range(ROWS // BATCH):

            def store(i, p, value, part=part):
                frame[p, part * BATCH + i : part * BATCH + i + 1, :] = value

            lookup(
                rows_table,
                [slots[b, n : n + 1, :] for n in range(part * BATCH, (part + 1) * BATCH)],
                store,
            )
        reflection(b, frame, phase, heading, coef)
        reflect(coef, field)
        total = None
        for part in range(ROWS // BATCH):
            lines = range(part * BATCH, (part + 1) * BATCH)
            more = gathered_sums([slots[b, n : n + 1, :] for n in lines], [field[n] for n in lines])
            total = more if total is None else total + more
        for hi in range(32):
            fields_send[2 * hi, b] = total[8 * hi : 8 * hi + 8, :LANES]
            fields_send[2 * hi + 1, b] = total[8 * hi : 8 * hi + 8, LANES:]

        @pl.loop(0, 8)
        def _(i):
            pair = i // 2
            kz = (1 - i % 2) * (4 + pair) + (i % 2) * (3 - pair)

            def give(dom):
                send(
                    fields_send.at[dom, b], fields_got.at[b, me],
                    fields_ssem.at[b], fields_rsem.at[b, pair], dom, my_bin,
                )

            each_of_plane((z + kz) % 8, i == 7, give)

        fields_got[b, me] = fields_send[me, b]

    for n in range(ROWS):
        exit_field[:, n * LANES : (n + 1) * LANES] = field[n]

    sums[...] = jnp.zeros_like(sums)

    @pl.loop(0, BOUNCES)
    def _(b):
        @pl.loop(0, 4)
        def _(pair):
            @pl.when(pair < 3)
            def _():
                await_bytes(fields_got.at[b, pl.ds(0, 16)], fields_rsem.at[b, pair])

            @pl.when(pair == 3)
            def _():
                await_bytes(fields_got.at[b, pl.ds(0, 15)], fields_rsem.at[b, 3])

            firsts = [((z + 8 - kz) % 8) * 8 for kz in (4 + pair, 3 - pair)]
            senders = [first + q for first in firsts for q in range(8)]
            total = gathered_sums(
                [ids_got[dom, pl.ds(b, 1), :] for dom in senders],
                [fields_got[b, dom] for dom in senders],
            )
            for j in range(2):
                sums[j] += total[:, LANES * j : LANES * (j + 1)]

    for k in range(1, BINS):
        other = (my_bin + k) % BINS
        send(
            sums.at[other // 2, pl.ds(pl.multiple_of((other % 2) * 128, 128), 128)],
            sums_got.at[k - 1],
            sums_sems.at[0, k - 1], sums_sems.at[1, k - 1], me, other,
        )
    mine = sums[my_bin // 2, pl.ds(pl.multiple_of((my_bin % 2) * 128, 128), 128), :]
    fetches[11].wait()
    for k in range(1, BINS):
        await_bytes(sums_got.at[k - 1], sums_sems.at[1, k - 1])
        mine = mine + sums_got[k - 1]
    mine = mine.astype(BF16)

    width = 512
    is_real = iota((8, width), 0) < 4
    for at in range(0, 1024, width):
        real, imag = jnp.zeros((8, width), F32), jnp.zeros((8, width), F32)
        for hi in range(8):
            left = jnp.concatenate(
                [mine[16 * hi : 16 * hi + 8], mine[16 * hi + 8 : 16 * hi + 16]], axis=1
            )
            lines = slice(256 * hi, 256 * (hi + 1))
            real = real + jnp.dot(left, held[0, lines, at : at + width], preferred_element_type=F32)
            imag = imag + jnp.dot(left, held[1, lines, at : at + width], preferred_element_type=F32)
        turned = pltpu.roll(imag, 4, 0)
        value = real + jnp.where(is_real, -turned, turned)
        for q in range(width // LANES):
            partial[at // LANES + q] = value[:, LANES * q : LANES * (q + 1)]

    @pl.loop(1, 8)
    def _(k):
        to = (z + k) % 8
        send(
            partial.at[to], along_got.at[z], along_sems.at[0], along_sems.at[1],
            to * 8 + me % 8, my_bin,
        )

    along_got[z] = partial[z]
    await_bytes(partial.at[pl.ds(0, 7)], along_sems.at[1])
    tile = along_got[0]
    for k in range(1, 8):
        tile = tile + along_got[k]
    piece[...] = tile
    spot = (me % 8) * BINS + my_bin

    @pl.loop(1, 32)
    def _(k):
        dom, bin_at = same_z(k)
        send(piece, last_got.at[spot], last_sems.at[0], last_sems.at[1], dom, bin_at)

    last_got[spot] = tile
    await_bytes(last_got.at[pl.ds(0, 31)], last_sems.at[1])
    tile = last_got[0]
    for k in range(1, 32):
        tile = tile + last_got[k]
    far[...] = tile

    await_bytes(ids_send.at[pl.ds(0, DOMS - 1)], ids_ssem)
    for h in range(HALVES):
        await_bytes(facts_send.at[h, pl.ds(0, DOMS - 1)], facts_ssem.at[h])
    for b in range(BOUNCES):
        await_bytes(fields_got.at[b, pl.ds(0, DOMS - 1)], fields_ssem.at[b])
    for k in range(1, BINS):
        await_bytes(sums_got.at[k - 1], sums_sems.at[0, k - 1])
    await_bytes(partial.at[pl.ds(0, 7)], along_sems.at[0])
    await_bytes(last_got.at[pl.ds(0, 31)], last_sems.at[0])


def main(*args):
    vmem = pltpu.VMEM
    dma = pltpu.SemaphoreType.DMA
    whole = pl.BlockSpec(memory_space=pltpu.VMEM)
    return pl.pallas_call(
        main_kernel,
        out_shape=(
            jax.ShapeDtypeStruct((8, LANES), F32),
            jax.ShapeDtypeStruct((8, ROWS * LANES), F32),
        ),
        in_specs=[pl.BlockSpec(memory_space=pltpu.HBM)] * 12,
        out_specs=(whole, whole),
        scratch_shapes=[
            vmem((2, 2048, 1024), BF16),
            vmem((BOUNCES, ROWS, LANES), I32),
            vmem((BOUNCES, ROWS * LANES), I32),
            vmem((BOUNCES, ROWS * LANES), F32),
            vmem((3, ROWS * LANES), F32),
            vmem((8, ROWS * LANES), F32),
            vmem((PARAMS, 64, LANES), F32),
            vmem((DOMS, BOUNCES, CAP), I32),
            vmem((DOMS, BOUNCES, CAP), I32),
            vmem((BOUNCES, ROWS, LANES), I32),
            vmem((2 * 32 * PARAMS, 256), BF16),
            vmem((HALVES, DOMS, PARAMS, EACH, CAP), F32),
            vmem((HALVES, DOMS, PARAMS, EACH, CAP), F32),
            vmem((PARAMS, ROWS, LANES), F32),
            vmem((BOUNCES, ROWS, LANES), F32),
            vmem((3, ROWS, LANES), F32),
            vmem((6, ROWS, LANES), F32),
            vmem((ROWS, 8, LANES), F32),
            vmem((DOMS, BOUNCES, 8, CAP), F32),
            vmem((BOUNCES, DOMS, 8, CAP), F32),
            vmem((2, 256, LANES), F32),
            vmem((BINS - 1, 128, LANES), F32),
            vmem((8, 8, LANES), F32),
            vmem((8, 8, LANES), F32),
            vmem((8, LANES), F32),
            vmem((32, 8, LANES), F32),
            dma((12,)),
            dma,
            dma((8,)),
            dma((HALVES,)),
            dma((HALVES,)),
            dma((BOUNCES,)),
            dma((BOUNCES, 4)),
            dma((2, BINS - 1)),
            dma((2,)),
            dma((2,)),
        ],
        compiler_params=pltpu.CompilerParams(
            collective_id=0, has_side_effects=True, vmem_limit_bytes=48 << 20
        ),
    )(*(pltpu.with_memory_space_constraint(a, pltpu.HBM) for a in args))


def body(
    field_in,
    heading_in,
    launch_domain,
    hop_domain,
    hit_facet,
    path_phase,
    facet_polar,
    facet_azimuth,
    facet_tilt,
    surface_resistance,
    surface_reactance,
    kernel,
):
    grid = (ROWS, LANES)
    params = (facet_polar, facet_azimuth, facet_tilt, surface_resistance, surface_reactance)
    far, exit_field = main(
        launch_domain.reshape(1, *grid),
        hop_domain.reshape(BOUNCES - 1, *grid),
        hit_facet,
        path_phase,
        heading_in,
        field_in,
        *(p.reshape(64, LANES) for p in params),
        kernel,
    )
    dom, bin_at = lax.axis_index("dom"), lax.axis_index("bin")
    spot = (dom % 8) * BINS + bin_at
    return lax.dynamic_slice_in_dim(far, spot * 4, 4, axis=1), exit_field


def solution(mesh):
    both = ("dom", "bin")
    in_specs = (
        P(None, both),
        P(None, both),
        P(both, None),
        P(None, both, None),
        P(None, both),
        P(None, both),
        P("dom"),
        P("dom"),
        P("dom"),
        P("dom"),
        P("dom"),
        P(None, both, None),
    )
    out_specs = (P(None, both), P(None, both))
    return jax.shard_map(body, mesh=mesh, in_specs=in_specs, out_specs=out_specs, check_vma=False)
```
